1024 devices in a mesh: slab: 32 (over z_lo, y), grid: 32 (over x, z_hi, core).
Axes of the slice: x: 4, y: 4, z: 32 (z_hi: 4, z_lo: 8; z = z_hi * 8 + z_lo), core: 2. Of those that a mesh axis runs over, the one named last changes fastest.
Arguments:
- orbitals: bfloat16 [64, 110592], P(None, 'grid'), may hold values from -6 to 6
- targets: int32 [64], replicated, may hold values from 0 to 63
- points: int32 [1024], P('slab'), may hold values from 0 to 110591, as said below
- fit: float32 [1024, 32], P('slab'), may hold values from -2 to 4, as said below
Outputs:
- applied_exchange: float32 [64, 110592], P('slab', 'grid')
The draws below stay inside these ranges and needn't reach their ends.
Inputs may be any that keep to these rules, and one draw needn't show every extreme that they name: `points`: 1024 distinct grid cells. `fit`: each block of 32 rows is a symmetric matrix.
All inputs are finite; a program needn't handle non-finite values.
Results may differ from the reference program's by a relative error of at most 0.004.
Values may be sent and summed in bfloat16 or wider, within the bound.
A program may use at most 32 MiB of HBM per device.

```python
import math
import jax
import jax.numpy as jnp
from jax import lax

NG = 48
NOCC = 64
CELLS = 110592
MU_GRP = 32
NMU = 1024
K = 64
N_SLAB = 32


def draw_points(key, part):
    key_inner, key_order = jax.random.split(key)
    interior = jax.random.permutation(key_inner, CELLS - 2)[:NMU - 2].astype(jnp.int32) + 1
    corners = jnp.array([0, CELLS - 1], dtype=jnp.int32)
    joined = jnp.concatenate([corners, interior])
    return jax.random.permutation(key_order, joined).astype(jnp.int32)


def draw_fit(key, part):
    key_diag, key_off = jax.random.split(key)
    blocks = NMU // MU_GRP
    spread = (6.0 / MU_GRP) ** 0.5
    diagonal = jnp.exp(jax.random.uniform(key_diag, (blocks, MU_GRP), jnp.float32, 0.0, 1.0986))
    noise = jax.random.uniform(key_off, (blocks, MU_GRP, MU_GRP), jnp.float32, -spread, spread)
    symmetric = 0.5 * (noise + jnp.swapaxes(noise, 1, 2))
    identity = jnp.eye(MU_GRP, dtype=jnp.float32)
    matrix = symmetric * (1.0 - identity) + identity * diagonal[:, :, None]
    return matrix.reshape(NMU, MU_GRP).astype(jnp.float32)


def plant(values, rng, low, top_value):
    dims = values.shape
    place = [jax.random.randint(jax.random.fold_in(rng, axis), (), 0, dims[axis]) for axis in range(len(dims))]
    values = values.at[tuple(place)].set(low)
    longest = dims.index(max(dims))
    place[longest] = (place[longest] + 1) % dims[longest]
    return values.at[tuple(place)].set(top_value)


def block_levels(key, dims, pieces, least, largest):
    level = 1.0
    for axis_at, parts in pieces:
        draws = jax.random.uniform(jax.random.fold_in(jax.random.fold_in(key, 6), axis_at), (parts,), jnp.float32, least / len(pieces), largest / len(pieces))
        level = level * jnp.repeat(jnp.exp(draws), dims[axis_at] // parts).reshape((-1,) + (1,) * (len(dims) - 1 - axis_at))
    return level


def bell_draw(own_key, shape, scale, most, shards=(), kind=jnp.bfloat16):
    drawn = scale * jax.random.normal(own_key, shape, jnp.float32)
    if shards:
        drawn = drawn * block_levels(own_key, shape, shards, -0.22, 0.18)
    return jnp.clip(drawn, -most, most).astype(kind)


def setup_inputs(seed: int = 0) -> dict:
    arg_keys = jax.random.split(jax.random.key(seed), 5)
    orbitals = bell_draw(arg_keys[0], (NOCC, CELLS), 1.0, 6.0, ((1, 32),))
    targets = plant(jax.random.randint(arg_keys[1], (K,), 0, NOCC), jax.random.fold_in(arg_keys[1], 1), 0, NOCC - 1).astype(jnp.int32)
    points = draw_points(jax.random.fold_in(arg_keys[4], 71), 0)
    fit = draw_fit(jax.random.fold_in(arg_keys[4], 71), 0)
    return dict(orbitals=orbitals, targets=targets, points=points, fit=fit)


screening = 4.0

def kernel_table():
    full_index = jnp.arange(NG)
    wrapped = jnp.where(full_index > NG // 2, full_index - NG, full_index).astype(jnp.float32)
    half_index = jnp.arange(NG // 2 + 1).astype(jnp.float32)
    step_size = 2.0 * math.pi / NG
    full_sq = wrapped * step_size * (wrapped * step_size)
    half_sq = half_index * step_size * (half_index * step_size)
    summed = full_sq[:, None, None] + full_sq[None, :, None] + half_sq[None, None, :]
    return screening / (screening + summed)

def screened(fields):
    cubes = fields.reshape(fields.shape[0], NG, NG, NG)
    spectrum = jnp.fft.rfftn(cubes, axes=(1, 2, 3)) * kernel_table()
    solved = jnp.fft.irfftn(spectrum, s=(NG, NG, NG), axes=(1, 2, 3))
    return solved.reshape(fields.shape).astype(jnp.float32)

def reference(orbitals, targets, points, fit):
    occupied = orbitals.shape[0]
    target_count = targets.shape[0]
    chosen = jnp.take(orbitals, targets, axis=0)
    point_blocks = points.reshape(N_SLAB, MU_GRP)
    fit_blocks = fit.reshape(N_SLAB, MU_GRP, MU_GRP)

    def one_group(running, item):
        block_points, block_fit = item
        at_points = jnp.take(orbitals, block_points, axis=1)
        target_points = jnp.take(at_points, targets, axis=0)
        density = jnp.dot(at_points.T, orbitals, preferred_element_type=jnp.float32) * (1.0 / math.sqrt(occupied))
        target_density = jnp.dot(target_points.T, chosen, preferred_element_type=jnp.float32) * (1.0 / math.sqrt(target_count))
        pairs = density * target_density
        fitted = jnp.dot(block_fit.T, pairs, precision=lax.Precision.HIGHEST).astype(jnp.bfloat16)
        fitted = lax.optimization_barrier(fitted)
        potential = screened(fitted.astype(jnp.float32)).astype(jnp.bfloat16)
        potential = lax.optimization_barrier(potential)
        weighted = (potential.astype(jnp.float32) * density).astype(jnp.bfloat16)
        return (running + jnp.dot(target_points, weighted, preferred_element_type=jnp.float32), None)
    initial = jnp.zeros((target_count, CELLS), jnp.float32)
    summed, unused = lax.scan(one_group, initial, (point_blocks, fit_blocks))
    return summed * (-1.0 / math.sqrt(NMU))
```

```python
import functools
import math

import jax
import jax.numpy as jnp
import numpy as np
from jax import lax
from jax.experimental import pallas as pl
from jax.experimental.pallas import tpu as pltpu
from jax.sharding import PartitionSpec as P

NG = 48
SCREENING = 4.0
MESH = pl.DeviceIdType.MESH
N_X, N_HI, N_CORE = 4, 4, 2
N_LO, N_Y = 8, 4
LANES = 128


def real_basis():
    rows, freq = [], []
    place = np.arange(NG)
    for m in range(NG // 2 + 1):
        scale = math.sqrt((1.0 if m in (0, NG // 2) else 2.0) / NG)
        rows.append(scale * np.cos(2.0 * math.pi * m * place / NG))
        freq.append(m)
    for m in range(1, NG // 2):
        rows.append(math.sqrt(2.0 / NG) * np.sin(2.0 * math.pi * m * place / NG))
        freq.append(m)
    return np.array(rows), np.array(freq)


BASIS, FREQ = real_basis()


def multiplier():
    sq = (2.0 * math.pi * FREQ / NG) ** 2
    return SCREENING / (SCREENING + sq[:, None, None] + sq[None, :, None] + sq[None, None, :])


def solve(vector):
    basis = jnp.asarray(BASIS, jnp.float32)
    weights = jnp.asarray(multiplier(), jnp.float32)
    cube = vector.reshape(NG, NG, NG).astype(jnp.float32)
    for pattern in ("xyz,mz->xym", "xyz,my->xmz", "xyz,mx->myz"):
        cube = jnp.einsum(pattern, cube, basis, precision=lax.Precision.HIGH)
    cube = cube * weights
    for pattern in ("myz,mx->xyz", "xmz,my->xyz", "xym,mz->xyz"):
        cube = jnp.einsum(pattern, cube, basis, precision=lax.Precision.HIGH)
    return cube.reshape(-1)


def greet(peers):
    barrier = pltpu.get_barrier_semaphore()
    for peer in peers:
        pl.semaphore_signal(barrier, inc=1, device_id=peer, device_id_type=MESH)
    pl.semaphore_wait(barrier, len(peers))


def push(src, dst, send, recv, peer):
    copy = pltpu.make_async_remote_copy(
        src_ref=src, dst_ref=dst, send_sem=send, recv_sem=recv, device_id=peer, device_id_type=MESH
    )
    copy.start()
    return copy


def points_kernel(mine_ref, out_ref, near, part, far, near_send, near_recv, far_send, far_recv):
    g = lax.axis_index("grid")
    core = lax.rem(g, N_CORE)
    hi = lax.rem(g // N_CORE, N_HI)
    x = g // (N_CORE * N_HI)

    def near_peer(dx, dc):
        return ((lax.rem(x + dx, N_X)) * N_HI + hi) * N_CORE + lax.rem(core + dc, N_CORE)

    def far_peer(dh):
        return (x * N_HI + lax.rem(hi + dh, N_HI)) * N_CORE + core

    near_steps = [(dx, dc) for dx in range(N_X) for dc in range(N_CORE) if dx or dc]
    greet([{"grid": near_peer(*step)} for step in near_steps] + [{"grid": far_peer(dh)} for dh in range(1, N_HI)])
    copies = [
        push(mine_ref, near.at[i], near_send.at[i], near_recv.at[i], {"grid": near_peer(*step)})
        for i, step in enumerate(near_steps)
    ]
    for copy in copies:
        copy.wait()
    total = mine_ref[...].astype(jnp.float32)
    for i in range(len(near_steps)):
        total = total + near[i].astype(jnp.float32)
    part[...] = total.astype(jnp.bfloat16)
    copies = [
        push(part, far.at[dh - 1], far_send.at[dh - 1], far_recv.at[dh - 1], {"grid": far_peer(dh)})
        for dh in range(1, N_HI)
    ]
    for copy in copies:
        copy.wait()
    for i in range(N_HI - 1):
        total = total + far[i].astype(jnp.float32)
    out_ref[...] = total.astype(jnp.bfloat16)


VMEM_SPEC = pl.BlockSpec(memory_space=pltpu.VMEM)


def sum_points(mine):
    near = N_X * N_CORE - 1
    far = N_HI - 1
    return pl.pallas_call(
        points_kernel,
        out_shape=jax.ShapeDtypeStruct(mine.shape, mine.dtype),
        in_specs=[VMEM_SPEC],
        out_specs=VMEM_SPEC,
        scratch_shapes=[
            pltpu.VMEM((near,) + mine.shape, mine.dtype),
            pltpu.VMEM(mine.shape, mine.dtype),
            pltpu.VMEM((far,) + mine.shape, mine.dtype),
            pltpu.SemaphoreType.DMA((near,)),
            pltpu.SemaphoreType.DMA((near,)),
            pltpu.SemaphoreType.DMA((far,)),
            pltpu.SemaphoreType.DMA((far,)),
        ],
        compiler_params=pltpu.CompilerParams(collective_id=0, has_side_effects=True),
        name="sum_points",
    )(mine)


def exchange_kernel(axis, n, stride, src_ref, out_ref, send, recv, local):
    index = lax.axis_index(axis)
    me = lax.rem(index // stride, n)
    base = index - me * stride

    def peer(d):
        return {axis: base + lax.rem(me + d, n) * stride}

    barrier = pltpu.get_barrier_semaphore()

    def hello(d, carry):
        pl.semaphore_signal(barrier, inc=1, device_id=peer(d), device_id_type=MESH)
        return carry

    lax.fori_loop(1, n, hello, 0)
    own = pltpu.make_async_copy(src_ref.at[me], out_ref.at[me], local)
    own.start()
    pl.semaphore_wait(barrier, n - 1)

    def describe(d):
        return pltpu.make_async_remote_copy(
            src_ref=src_ref.at[lax.rem(me + d, n)],
            dst_ref=out_ref.at[me],
            send_sem=send.at[d],
            recv_sem=recv.at[d],
            device_id=peer(d),
            device_id_type=MESH,
        )

    def begin(d, carry):
        describe(d).start()
        return carry

    def finish(d, carry):
        copy = describe(d)
        copy.wait_send()
        copy.wait_recv()
        return carry

    lax.fori_loop(1, n, begin, 0)
    own.wait()
    lax.fori_loop(1, n, finish, 0)


def exchange(blocks, axis, n, stride, ident, name):
    return pl.pallas_call(
        functools.partial(exchange_kernel, axis, n, stride),
        out_shape=jax.ShapeDtypeStruct(blocks.shape, blocks.dtype),
        in_specs=[VMEM_SPEC],
        out_specs=VMEM_SPEC,
        scratch_shapes=[
            pltpu.SemaphoreType.DMA((n,)),
            pltpu.SemaphoreType.DMA((n,)),
            pltpu.SemaphoreType.DMA,
        ],
        compiler_params=pltpu.CompilerParams(collective_id=ident, has_side_effects=True),
        name=name,
    )(blocks)


def body(orbitals, targets, points, fit):
    occupied, shard_len = orbitals.shape
    target_count = targets.shape[0]
    group_size = points.shape[0]
    n_grid = N_X * N_HI * N_CORE
    slab_count = N_LO * N_Y
    tiles = shard_len // LANES
    rows_each = target_count // slab_count
    offsets = points - lax.axis_index("grid") * shard_len
    cell_ids = lax.broadcasted_iota(jnp.int32, (group_size, shard_len), 1)
    one_hot = (cell_ids == offsets[:, None]).astype(jnp.bfloat16)
    terms = lax.dot_general(
        one_hot, orbitals, (((1,), (1,)), ((), ())), preferred_element_type=jnp.float32
    ).astype(jnp.bfloat16)
    at_points = sum_points(terms)
    choose = (lax.broadcasted_iota(jnp.int32, (occupied, target_count), 0) == targets[None, :]).astype(jnp.bfloat16)
    target_points = jnp.dot(at_points, choose, preferred_element_type=jnp.float32).astype(jnp.bfloat16)
    density = jnp.dot(at_points, orbitals, preferred_element_type=jnp.float32) * (1.0 / math.sqrt(occupied))
    chosen = lax.dot_general(
        choose, orbitals, (((0,), (0,)), ((), ())), preferred_element_type=jnp.float32
    ).astype(jnp.bfloat16)
    target_density = jnp.dot(target_points, chosen, preferred_element_type=jnp.float32) * (
        1.0 / math.sqrt(target_count)
    )
    pairs = density * target_density
    fitted = lax.dot_general(
        fit, pairs, (((0,), (0,)), ((), ())), precision=lax.Precision.HIGHEST, preferred_element_type=jnp.float32
    ).astype(jnp.bfloat16)
    vectors = exchange(fitted.reshape(n_grid, tiles, LANES), "grid", n_grid, 1, 1, "spread")
    potential = solve(vectors).astype(jnp.bfloat16)
    returned = exchange(potential.reshape(n_grid, tiles, LANES), "grid", n_grid, 1, 2, "collect")
    returned = returned.reshape(group_size, shard_len)
    weighted = (returned.astype(jnp.float32) * density).astype(jnp.bfloat16)
    ordered = target_points.reshape(group_size, N_LO, N_Y, rows_each).transpose(0, 2, 1, 3).reshape(group_size, -1)
    partial = lax.dot_general(
        ordered, weighted, (((0,), (0,)), ((), ())), preferred_element_type=jnp.float32
    ).astype(jnp.bfloat16)
    by_y = exchange(partial.reshape(N_Y, -1, shard_len), "slab", N_Y, 1, 3, "sum_y")
    half = jnp.sum(by_y.astype(jnp.float32), axis=0).astype(jnp.bfloat16)
    by_lo = exchange(half.reshape(N_LO, rows_each * tiles, LANES), "slab", N_LO, N_Y, 4, "sum_lo")
    summed = jnp.sum(by_lo.astype(jnp.float32), axis=0).reshape(rows_each, shard_len)
    return summed * (-1.0 / math.sqrt(group_size * slab_count))


def solution(mesh):
    in_specs = (P(None, "grid"), P(), P("slab"), P("slab", None))
    out_specs = P("slab", "grid")
    return jax.shard_map(body, mesh=mesh, in_specs=in_specs, out_specs=out_specs, check_vma=False)
```

```python
import functools
import math

import jax
import jax.numpy as jnp
import numpy as np
from jax import lax
from jax.experimental import pallas as pl
from jax.experimental.pallas import tpu as pltpu
from jax.sharding import PartitionSpec as P

NG = 48
SCREENING = 4.0
MESH = pl.DeviceIdType.MESH
N_X, N_HI, N_CORE = 4, 4, 2
N_LO, N_Y = 8, 4
N_GRID = N_X * N_HI * N_CORE
LANES = 128
SLOT = 32
F32, BF16 = jnp.float32, jnp.bfloat16


def real_basis():
    rows, freq = [], []
    place = np.arange(NG)
    for m in range(NG // 2 + 1):
        scale = math.sqrt((1.0 if m in (0, NG // 2) else 2.0) / NG)
        rows.append(scale * np.cos(2.0 * math.pi * m * place / NG))
        freq.append(m)
    for m in range(1, NG // 2):
        rows.append(math.sqrt(2.0 / NG) * np.sin(2.0 * math.pi * m * place / NG))
        freq.append(m)
    return np.array(rows), np.array(freq)


def split_table(table):
    high = table.astype(BF16)
    low = (table - high.astype(np.float64)).astype(BF16)
    return high, low


def tables():
    basis, freq = real_basis()
    left = []
    for matrix in (basis, basis.T):
        high, low = split_table(matrix)
        left.append(np.concatenate([high, high, low], axis=1))
    lines = np.zeros((2 * NG, LANES), BF16)
    high, low = split_table(basis.T)
    lines[:NG, :NG] = high
    lines[NG:, :NG] = low
    square = ((2.0 * math.pi * freq / NG) ** 2).astype(np.float32)
    column = np.broadcast_to(square[:, None], (NG, LANES)).copy()
    row = np.zeros((8, LANES), np.float32)
    row[:, :NG] = square
    return np.stack(left), lines, np.concatenate([column, row])


def stack(values):
    high = values.astype(BF16)
    low = (values - high.astype(F32)).astype(BF16)
    return jnp.concatenate([high, low, high], axis=0)


def dot(a, b):
    return jnp.dot(a, b, preferred_element_type=F32)


def dot_nt(a, b):
    return lax.dot_general(a, b, (((1,), (1,)), ((), ())), preferred_element_type=F32)


def column_of(row, count):
    same = lax.broadcasted_iota(jnp.int32, (count, count), 0) == lax.broadcasted_iota(jnp.int32, (count, count), 1)
    return jnp.sum(jnp.where(same, row, 0), axis=1, keepdims=True)


def spans(line):
    return range(line * NG // LANES, (line * NG + NG - 1) // LANES + 1)


def kernel(
    occupied, targets_n, group, shard, orb_ref, targets_ref, points_ref, fit_ref, left_ref, lines_ref, square_ref,
    out_ref, mine, near, part, far, chosen, density, flat, packed, cells, cube, weights, zline,
    send_a, recv_a, send_b, recv_b, y_out, y_in, lo_flat, lo_out, lo_in, last,
    near_s, near_r, far_s, far_r, a_s, a_r, b_s, b_r, y_s, y_r, lo_s, lo_r, local,
):
    grid, slab = lax.axis_index("grid"), lax.axis_index("slab")
    core, hi, x = lax.rem(grid, N_CORE), lax.rem(grid // N_CORE, N_HI), grid // (N_CORE * N_HI)
    lo, y = slab // N_Y, lax.rem(slab, N_Y)
    tiles = shard // LANES
    rows = tiles // 3
    wire = tiles + tiles % 2
    each = targets_n // (N_LO * N_Y)

    def grid_peer(dx, dh, dc):
        return (lax.rem(x + dx, N_X) * N_HI + lax.rem(hi + dh, N_HI)) * N_CORE + lax.rem(core + dc, N_CORE)

    def y_peer(d):
        return lo * N_Y + lax.rem(y + d, N_Y)

    def lo_peer(d):
        return lax.rem(lo + d, N_LO) * N_Y + y

    offsets = [(dx, dh, dc) for dh in (2, 1, 3, 0) for dx in range(N_X) for dc in range(N_CORE) if dx or dh or dc]
    barrier = pltpu.get_barrier_semaphore()
    for step in offsets:
        pl.semaphore_signal(barrier, inc=1, device_id={"grid": grid_peer(*step)}, device_id_type=MESH)
    for d in range(1, N_Y):
        pl.semaphore_signal(barrier, inc=1, device_id={"slab": y_peer(d)}, device_id_type=MESH)
    for d in range(1, N_LO):
        pl.semaphore_signal(barrier, inc=1, device_id={"slab": lo_peer(d)}, device_id_type=MESH)

    def push(src, dst, send, recv, peer):
        copy = pltpu.make_async_remote_copy(
            src_ref=src, dst_ref=dst, send_sem=send, recv_sem=recv, device_id=peer, device_id_type=MESH
        )
        copy.start()
        return copy

    offset = column_of(points_ref[...], group) - grid * shard
    for i in range(rows):
        ids = lax.broadcasted_iota(jnp.int32, (group, 384), 1) + i * 384
        term = dot_nt(
            jnp.where(ids == offset, 1.0, 0.0).astype(BF16), orb_ref[:, i * 384 : (i + 1) * 384]
        )
        total = term if i == 0 else total + term
    mine[...] = total.astype(BF16)
    targets = targets_ref[...]
    occ = lax.broadcasted_iota(jnp.int32, (occupied, targets_n), 0)
    choose = jnp.where(occ == targets, 1.0, 0.0).astype(BF16)
    pick = jnp.where(
        lax.broadcasted_iota(jnp.int32, (targets_n, occupied), 1) == column_of(targets, targets_n), 1.0, 0.0
    ).astype(BF16)
    new = lax.broadcasted_iota(jnp.int32, (targets_n, targets_n), 0)
    old = lax.broadcasted_iota(jnp.int32, (targets_n, targets_n), 1)
    from_old = ((new // each) % N_LO) * (N_Y * each) + (new // (each * N_LO)) * each + new % each
    reorder = dot(jnp.where(old == from_old, 1.0, 0.0).astype(BF16), pick).astype(BF16)
    for i in range(rows):
        chosen[:, i * 384 : (i + 1) * 384] = dot(pick, orb_ref[:, i * 384 : (i + 1) * 384]).astype(BF16)
    zline[...] = jnp.zeros_like(zline)
    for line in range(8):
        at = slice(line * NG, (line + 1) * NG)
        for k in range(2):
            zline[k, at, line * LANES : (line + 1) * LANES] = lines_ref[k * NG : (k + 1) * NG, :]
    flat[...] = jnp.zeros_like(flat)
    lo_flat[...] = jnp.zeros_like(lo_flat)
    column, row = square_ref[:NG, :], square_ref[NG : NG + 1, :]

    def weigh(m, carry):
        one = square_ref[pl.ds(m, 1), :]
        weights[pl.ds(pl.multiple_of(m * NG, NG), NG), :] = SCREENING / (SCREENING + column + row + one[:, :1])
        return carry

    lax.fori_loop(0, NG, weigh, 0)
    fit = fit_ref[...]
    fit_1 = fit.astype(BF16)
    fit_2 = (fit - fit_1.astype(F32)).astype(BF16)
    fit_3 = (fit - fit_1.astype(F32) - fit_2.astype(F32)).astype(BF16)
    fits = jnp.concatenate([fit_1, fit_1, fit_2, fit_1, fit_2, fit_3], axis=1)

    pl.semaphore_wait(barrier, len(offsets) + N_Y - 1 + N_LO - 1)

    near_steps = [(dx, 0, dc) for dx in range(N_X) for dc in range(N_CORE) if dx or dc]
    copies = [
        push(mine, near.at[i], near_s.at[i], near_r.at[i], {"grid": grid_peer(*step)})
        for i, step in enumerate(near_steps)
    ]
    for copy in copies:
        copy.wait()
    total = mine[...].astype(F32)
    for i in range(len(near_steps)):
        total = total + near[i].astype(F32)
    part[...] = total.astype(BF16)
    copies = [
        push(part, far.at[d - 1], far_s.at[d - 1], far_r.at[d - 1], {"grid": grid_peer(0, d, 0)})
        for d in range(1, N_HI)
    ]
    for copy in copies:
        copy.wait()
    for i in range(N_HI - 1):
        total = total + far[i].astype(F32)
    at_points = total.astype(BF16)

    target_points = dot(at_points, choose).astype(BF16)
    ordered = dot_nt(reorder, at_points).astype(BF16)
    for i in range(rows):
        at = slice(i * 384, (i + 1) * 384)
        dense = dot(at_points, orb_ref[:, at]) * (1.0 / math.sqrt(occupied))
        density[:, at] = dense
        pair = dense * (dot(target_points, chosen[:, at]) * (1.0 / math.sqrt(targets_n)))
        pair_1 = pair.astype(BF16)
        rest = pair - pair_1.astype(F32)
        pair_2 = rest.astype(BF16)
        pair_3 = (rest - pair_2.astype(F32)).astype(BF16)
        fitted = dot(fits, jnp.concatenate([pair_1, pair_2, pair_1, pair_3, pair_2, pair_1], axis=0))
        for t in range(3):
            flat[pl.ds(3 * i + t, group, stride=SLOT), :] = fitted[:, t * LANES : (t + 1) * LANES]
    send_a[...] = flat[...].reshape(N_GRID, SLOT, LANES).astype(BF16)

    def spread(source, target, send, recv):
        own = pltpu.make_async_copy(source.at[grid], target.at[grid], local)
        own.start()
        copies = []
        for i, step in enumerate(offsets):
            peer = grid_peer(*step)
            copies.append(
                push(
                    source.at[peer, pl.ds(0, wire)], target.at[grid, pl.ds(0, wire)], send.at[i], recv.at[i],
                    {"grid": peer},
                )
            )
        own.wait()
        for copy in copies:
            copy.wait()
        flat[...] = target[...].astype(F32).reshape(N_GRID * SLOT, LANES)

    spread(send_a, recv_a, a_s, a_r)

    for i in range(rows):
        for t in range(3):
            packed[i * N_GRID : (i + 1) * N_GRID, t * LANES : (t + 1) * LANES] = flat[
                pl.ds(3 * i + t, N_GRID, stride=SLOT), :
            ].astype(BF16)
    for line in range(8):
        at = slice(line * LANES, (line + 1) * LANES)
        got = None
        for t in spans(line):
            lanes = slice(t * LANES, (t + 1) * LANES)
            for k in range(2):
                term = dot(packed[:, lanes], zline[k, lanes, at])
                got = term if got is None else got + term
        for i in range(rows):
            cube[pl.ds(8 * i + line, N_GRID, stride=8 * rows), :] = got[i * N_GRID : (i + 1) * N_GRID, :]

    many = 8

    def along_y(which):
        def one(step, carry):
            for u in range(0, many, 2):
                first = pl.ds(pl.multiple_of((step * many + u) * NG, NG), NG)
                second = pl.ds(pl.multiple_of((step * many + u + 1) * NG, NG), NG)
                both = jnp.concatenate([stack(cube[first, :]), stack(cube[second, :])], axis=1)
                got = dot(left_ref[which], both)
                cube[first, :] = got[:, :LANES]
                cube[second, :] = got[:, LANES:]
            return carry

        lax.fori_loop(0, NG // many, one, 0)

    def along_x(step, carry):
        for u in range(0, many, 2):
            first, second = step * many + u, step * many + u + 1
            at = [pl.ds(m, NG, stride=NG) for m in (first, second)]
            both = jnp.concatenate([stack(cube[at[0], :]), stack(cube[at[1], :])], axis=1)
            got = dot(left_ref[0], both)
            got = [
                got[:, k * LANES : (k + 1) * LANES] * weights[pl.ds(pl.multiple_of(m * NG, NG), NG), :]
                for k, m in enumerate((first, second))
            ]
            got = dot(left_ref[1], jnp.concatenate([stack(got[0]), stack(got[1])], axis=1))
            cube[at[0], :] = got[:, :LANES]
            cube[at[1], :] = got[:, LANES:]
        return carry

    along_y(0)
    lax.fori_loop(0, NG // many, along_x, 0)
    along_y(1)
    tile = [None, None, None]
    for line in range(8):
        at = slice(line * LANES, (line + 1) * LANES)
        for i in range(rows):
            cells[i * N_GRID : (i + 1) * N_GRID, :] = cube[pl.ds(8 * i + line, N_GRID, stride=8 * rows), :]
        value = cells[...]
        high = value.astype(BF16)
        low = (value - high.astype(F32)).astype(BF16)
        for t in spans(line):
            lanes = slice(t * LANES, (t + 1) * LANES)
            term = dot_nt(high, zline[0, lanes, at]) + dot_nt(low, zline[0, lanes, at])
            term = term + dot_nt(high, zline[1, lanes, at])
            tile[t] = term if tile[t] is None else tile[t] + term
    for i in range(rows):
        for t in range(3):
            flat[pl.ds(3 * i + t, N_GRID, stride=SLOT), :] = tile[t][i * N_GRID : (i + 1) * N_GRID, :]
    send_b[...] = flat[...].reshape(N_GRID, SLOT, LANES).astype(BF16)

    spread(send_b, recv_b, b_s, b_r)

    for i in range(rows):
        at = slice(i * 384, (i + 1) * 384)
        got = jnp.concatenate([flat[pl.ds(3 * i + t, group, stride=SLOT), :] for t in range(3)], axis=1)
        weighted = (got * density[:, at]).astype(BF16)
        y_out[:, :, at] = dot(ordered, weighted).astype(BF16).reshape(N_Y, targets_n // N_Y, 384)
    copies = [
        push(y_out.at[lax.rem(y + d, N_Y)], y_in.at[d - 1], y_s.at[d - 1], y_r.at[d - 1], {"slab": y_peer(d)})
        for d in range(1, N_Y)
    ]
    for copy in copies:
        copy.wait()
    for i in range(rows):
        at = slice(i * 384, (i + 1) * 384)
        total = y_out[y, :, at].astype(F32)
        for d in range(N_Y - 1):
            total = total + y_in[d, :, at].astype(F32)
        for t in range(3):
            lo_flat[pl.ds(3 * i + t, N_LO * each, stride=SLOT), :] = total[:, t * LANES : (t + 1) * LANES]
    lo_out[...] = lo_flat[...].reshape(N_LO, each, SLOT, LANES).astype(BF16)
    copies = [
        push(
            lo_out.at[lax.rem(lo + d, N_LO), :, pl.ds(0, wire)], lo_in.at[d - 1, :, pl.ds(0, wire)],
            lo_s.at[d - 1], lo_r.at[d - 1], {"slab": lo_peer(d)},
        )
        for d in range(1, N_LO)
    ]
    for copy in copies:
        copy.wait()
    total = lo_out[lo].astype(F32)
    for d in range(N_LO - 1):
        total = total + lo_in[d].astype(F32)
    last[...] = (total * (-1.0 / math.sqrt(group * N_LO * N_Y))).reshape(each * SLOT, LANES)
    for c in range(tiles):
        out_ref[:, c * LANES : (c + 1) * LANES] = last[pl.ds(c, each, stride=SLOT), :]


def body(orbitals, targets, points, fit):
    occupied, shard = orbitals.shape
    targets_n, group = targets.shape[0], points.shape[0]
    each = targets_n // (N_LO * N_Y)
    left, lines, square = tables()
    near, far = N_X * N_CORE - 1, N_HI - 1
    peers = N_GRID - 1
    dma = pltpu.SemaphoreType.DMA
    vmem = pltpu.VMEM
    return pl.pallas_call(
        functools.partial(kernel, occupied, targets_n, group, shard),
        out_shape=jax.ShapeDtypeStruct((each, shard), F32),
        in_specs=[pl.BlockSpec(memory_space=pltpu.VMEM)] * 7,
        out_specs=pl.BlockSpec(memory_space=pltpu.VMEM),
        scratch_shapes=[
            vmem((group, occupied), BF16),
            vmem((near, group, occupied), BF16),
            vmem((group, occupied), BF16),
            vmem((far, group, occupied), BF16),
            vmem((targets_n, shard), BF16),
            vmem((group, shard), F32),
            vmem((N_GRID * SLOT, LANES), F32),
            vmem((N_GRID * shard // 384, 384), BF16),
            vmem((N_GRID * shard // 384, LANES), F32),
            vmem((NG * NG, LANES), F32),
            vmem((NG * NG, LANES), F32),
            vmem((2, 384, 8 * LANES), BF16),
            vmem((N_GRID, SLOT, LANES), BF16),
            vmem((N_GRID, SLOT, LANES), BF16),
            vmem((N_GRID, SLOT, LANES), BF16),
            vmem((N_GRID, SLOT, LANES), BF16),
            vmem((N_Y, targets_n // N_Y, shard), BF16),
            vmem((N_Y - 1, targets_n // N_Y, shard), BF16),
            vmem((N_LO * each * SLOT, LANES), F32),
            vmem((N_LO, each, SLOT, LANES), BF16),
            vmem((N_LO - 1, each, SLOT, LANES), BF16),
            vmem((each * SLOT, LANES), F32),
            dma((near,)), dma((near,)), dma((far,)), dma((far,)),
            dma((peers,)), dma((peers,)), dma((peers,)), dma((peers,)),
            dma((N_Y - 1,)), dma((N_Y - 1,)), dma((N_LO - 1,)), dma((N_LO - 1,)), dma,
        ],
        compiler_params=pltpu.CompilerParams(collective_id=0, has_side_effects=True, vmem_limit_bytes=40 << 20),
        name="exchange_operator",
    )(
        orbitals, targets.reshape(1, -1), points.reshape(1, -1), fit,
        jnp.asarray(left), jnp.asarray(lines), jnp.asarray(square),
    )


def solution(mesh):
    in_specs = (P(None, "grid"), P(), P("slab"), P("slab", None))
    out_specs = P("slab", "grid")
    return jax.shard_map(body, mesh=mesh, in_specs=in_specs, out_specs=out_specs, check_vma=False)
```

```python
import functools
import math

import jax
import jax.numpy as jnp
import numpy as np
from jax import lax
from jax.experimental import pallas as pl
from jax.experimental.pallas import tpu as pltpu
from jax.sharding import PartitionSpec as P

NG = 48
SCREENING = 4.0
MESH = pl.DeviceIdType.MESH
N_X, N_HI, N_CORE = 4, 4, 2
N_LO, N_Y = 8, 4
N_GRID = N_X * N_HI * N_CORE
LANES = 128
SLOT = 32
PIECE = 16
F32, BF16 = jnp.float32, jnp.bfloat16


def real_basis():
    rows, freq = [], []
    place = np.arange(NG)
    for m in range(NG // 2 + 1):
        scale = math.sqrt((1.0 if m in (0, NG // 2) else 2.0) / NG)
        rows.append(scale * np.cos(2.0 * math.pi * m * place / NG))
        freq.append(m)
    for m in range(1, NG // 2):
        rows.append(math.sqrt(2.0 / NG) * np.sin(2.0 * math.pi * m * place / NG))
        freq.append(m)
    return np.array(rows), np.array(freq)


def split_table(table):
    high = table.astype(BF16)
    low = (table - high.astype(np.float64)).astype(BF16)
    return high, low


def tables():
    basis, freq = real_basis()
    left = []
    for matrix in (basis, basis.T):
        high, low = split_table(matrix)
        left.append(np.concatenate([high, high, low], axis=1))
    lines = np.zeros((2 * NG, LANES), BF16)
    high, low = split_table(basis.T)
    lines[:NG, :NG] = high
    lines[NG:, :NG] = low
    square = ((2.0 * math.pi * freq / NG) ** 2).astype(np.float32)
    column = np.broadcast_to(square[:, None], (NG, LANES)).copy()
    row = np.zeros((8, LANES), np.float32)
    row[:, :NG] = square
    return np.stack(left), lines, np.concatenate([column, row])


def stack(values):
    high = values.astype(BF16)
    low = (values - high.astype(F32)).astype(BF16)
    return jnp.concatenate([high, low, high], axis=0)


def dot(a, b):
    return jnp.dot(a, b, preferred_element_type=F32)


def dot_nt(a, b):
    return lax.dot_general(a, b, (((1,), (1,)), ((), ())), preferred_element_type=F32)


def column_of(row, count):
    same = lax.broadcasted_iota(jnp.int32, (count, count), 0) == lax.broadcasted_iota(jnp.int32, (count, count), 1)
    return jnp.sum(jnp.where(same, row, 0), axis=1, keepdims=True)


def row_of(tile):
    return tile + (tile >= PIECE - 1)


def spans(line):
    return range(line * NG // LANES, (line * NG + NG - 1) // LANES + 1)


def kernel(
    occupied, targets_n, group, shard, orb_hbm, targets_hbm, points_hbm, fit_hbm, left_hbm, lines_hbm, square_hbm,
    out_ref, orb_ref, targets_ref, points_ref, fit_ref, left_ref, lines_ref, square_ref, mine, near, part, far, chosen, density, flat, packed, cells, cube, weights, zline,
    send_a, recv_a, send_b, recv_b, y_out, y_in, lo_flat, lo_out, lo_in, last,
    near_s, near_r, far_s, far_r, a_s, a_r, b_s, b_r, y_s, y_r, lo_s, lo_r, local, fetched,
):
    grid, slab = lax.axis_index("grid"), lax.axis_index("slab")
    core, hi, x = lax.rem(grid, N_CORE), lax.rem(grid // N_CORE, N_HI), grid // (N_CORE * N_HI)
    lo, y = slab // N_Y, lax.rem(slab, N_Y)
    tiles = shard // LANES
    rows = tiles // 3
    wire = row_of(tiles - 1) + 1
    pieces = [(0, PIECE, range((PIECE - 1) // 3)), (PIECE, wire, range((PIECE - 1) // 3, rows))]
    each = targets_n // (N_LO * N_Y)

    def grid_peer(dx, dh, dc):
        return (lax.rem(x + dx, N_X) * N_HI + lax.rem(hi + dh, N_HI)) * N_CORE + lax.rem(core + dc, N_CORE)

    def y_peer(d):
        return lo * N_Y + lax.rem(y + d, N_Y)

    def lo_peer(d):
        return lax.rem(lo + d, N_LO) * N_Y + y

    offsets = [(dx, dh, dc) for dx in (2, 1, 3, 0) for dc in (1, 0) for dh in (2, 1, 3, 0) if dx or dh or dc]
    fetches = [
        pltpu.make_async_copy(source, target, fetched.at[i])
        for i, (source, target) in enumerate(
            [
                (points_hbm, points_ref), (orb_hbm, orb_ref), (targets_hbm, targets_ref), (lines_hbm, lines_ref),
                (square_hbm, square_ref), (fit_hbm, fit_ref), (left_hbm, left_ref),
            ]
        )
    ]
    barrier = pltpu.get_barrier_semaphore()
    for step in offsets:
        pl.semaphore_signal(barrier, inc=1, device_id={"grid": grid_peer(*step)}, device_id_type=MESH)
    for d in range(1, N_Y):
        pl.semaphore_signal(barrier, inc=1, device_id={"slab": y_peer(d)}, device_id_type=MESH)
    for d in range(1, N_LO):
        pl.semaphore_signal(barrier, inc=1, device_id={"slab": lo_peer(d)}, device_id_type=MESH)

    for fetch in fetches:
        fetch.start()

    def push(src, dst, send, recv, peer):
        copy = pltpu.make_async_remote_copy(
            src_ref=src, dst_ref=dst, send_sem=send, recv_sem=recv, device_id=peer, device_id_type=MESH
        )
        copy.start()
        return copy

    flat[...] = jnp.zeros_like(flat)
    lo_flat[...] = jnp.zeros_like(lo_flat)
    zline[...] = jnp.zeros_like(zline)
    for fetch in fetches:
        fetch.wait()
    offset = column_of(points_ref[...], group) - grid * shard
    for i in range(rows):
        ids = lax.broadcasted_iota(jnp.int32, (group, 384), 1) + i * 384
        term = dot_nt(
            jnp.where(ids == offset, 1.0, 0.0).astype(BF16), orb_ref[:, i * 384 : (i + 1) * 384]
        )
        total = term if i == 0 else total + term
    mine[...] = total.astype(BF16)
    targets = targets_ref[...]
    occ = lax.broadcasted_iota(jnp.int32, (occupied, targets_n), 0)
    choose = jnp.where(occ == targets, 1.0, 0.0).astype(BF16)
    pick = jnp.where(
        lax.broadcasted_iota(jnp.int32, (targets_n, occupied), 1) == column_of(targets, targets_n), 1.0, 0.0
    ).astype(BF16)
    new = lax.broadcasted_iota(jnp.int32, (targets_n, targets_n), 0)
    old = lax.broadcasted_iota(jnp.int32, (targets_n, targets_n), 1)
    from_old = ((new // each) % N_LO) * (N_Y * each) + (new // (each * N_LO)) * each + new % each
    reorder = dot(jnp.where(old == from_old, 1.0, 0.0).astype(BF16), pick).astype(BF16)
    for i in range(rows):
        chosen[:, i * 384 : (i + 1) * 384] = dot(pick, orb_ref[:, i * 384 : (i + 1) * 384]).astype(BF16)
    for line in range(8):
        at = slice(line * NG, (line + 1) * NG)
        for k in range(2):
            zline[k, at, line * LANES : (line + 1) * LANES] = lines_ref[k * NG : (k + 1) * NG, :]
    column, row = square_ref[:NG, :], square_ref[NG : NG + 1, :]

    def weigh(m, carry):
        one = square_ref[pl.ds(m, 1), :]
        weights[pl.ds(pl.multiple_of(m * NG, NG), NG), :] = SCREENING / (SCREENING + column + row + one[:, :1])
        return carry

    lax.fori_loop(0, NG, weigh, 0)
    fit = fit_ref[...]
    fit_1 = fit.astype(BF16)
    fit_2 = (fit - fit_1.astype(F32)).astype(BF16)
    fit_3 = (fit - fit_1.astype(F32) - fit_2.astype(F32)).astype(BF16)
    fits = jnp.concatenate([fit_1, fit_1, fit_2, fit_1, fit_2, fit_3], axis=1)

    pl.semaphore_wait(barrier, len(offsets) + N_Y - 1 + N_LO - 1)

    near_steps = [(dx, 0, dc) for dx in range(N_X) for dc in range(N_CORE) if dx or dc]
    copies = [
        push(mine, near.at[i], near_s.at[i], near_r.at[i], {"grid": grid_peer(*step)})
        for i, step in enumerate(near_steps)
    ]
    for copy in copies:
        copy.wait()
    total = mine[...].astype(F32)
    for i in range(len(near_steps)):
        total = total + near[i].astype(F32)
    part[...] = total.astype(BF16)
    copies = [
        push(part, far.at[d - 1], far_s.at[d - 1], far_r.at[d - 1], {"grid": grid_peer(0, d, 0)})
        for d in range(1, N_HI)
    ]
    for copy in copies:
        copy.wait()
    for i in range(N_HI - 1):
        total = total + far[i].astype(F32)
    at_points = total.astype(BF16)

    target_points = dot(at_points, choose).astype(BF16)
    ordered = dot_nt(reorder, at_points).astype(BF16)
    for i in range(rows):
        at = slice(i * 384, (i + 1) * 384)
        dense = dot(at_points, orb_ref[:, at]) * (1.0 / math.sqrt(occupied))
        density[:, at] = dense
        pair = dense * (dot(target_points, chosen[:, at]) * (1.0 / math.sqrt(targets_n)))
        pair_1 = pair.astype(BF16)
        rest = pair - pair_1.astype(F32)
        pair_2 = rest.astype(BF16)
        pair_3 = (rest - pair_2.astype(F32)).astype(BF16)
        fitted = dot(fits, jnp.concatenate([pair_1, pair_2, pair_1, pair_3, pair_2, pair_1], axis=0))
        for t in range(3):
            flat[pl.ds(row_of(3 * i + t), group, stride=SLOT), :] = fitted[:, t * LANES : (t + 1) * LANES]
    send_a[...] = flat[...].reshape(N_GRID, SLOT, LANES).astype(BF16)

    def spread(source, target, send, recv, first, past):
        copies = []
        for i, step in enumerate(offsets):
            peer = grid_peer(*step)
            copies.append(
                push(
                    source.at[peer, pl.ds(first, past - first)], target.at[grid, pl.ds(first, past - first)],
                    send.at[i], recv.at[i], {"grid": peer},
                )
            )
        return copies

    own = pltpu.make_async_copy(send_a.at[grid], recv_a.at[grid], local)
    copies = spread(send_a, recv_a, a_s, a_r, 0, wire)
    own.start()
    own.wait()
    for copy in copies:
        copy.wait()
    flat[...] = recv_a[...].astype(F32).reshape(N_GRID * SLOT, LANES)

    for i in range(rows):
        for t in range(3):
            packed[i * N_GRID : (i + 1) * N_GRID, t * LANES : (t + 1) * LANES] = flat[
                pl.ds(row_of(3 * i + t), N_GRID, stride=SLOT), :
            ].astype(BF16)
    for line in range(8):
        at = slice(line * LANES, (line + 1) * LANES)
        got = None
        for t in spans(line):
            lanes = slice(t * LANES, (t + 1) * LANES)
            for k in range(2):
                term = dot(packed[:, lanes], zline[k, lanes, at])
                got = term if got is None else got + term
        for i in range(rows):
            cube[pl.ds(8 * i + line, N_GRID, stride=8 * rows), :] = got[i * N_GRID : (i + 1) * N_GRID, :]

    many = 8

    def along_y(which):
        def one(step, carry):
            for u in range(0, many, 2):
                first = pl.ds(pl.multiple_of((step * many + u) * NG, NG), NG)
                second = pl.ds(pl.multiple_of((step * many + u + 1) * NG, NG), NG)
                both = jnp.concatenate([stack(cube[first, :]), stack(cube[second, :])], axis=1)
                got = dot(left_ref[which], both)
                cube[first, :] = got[:, :LANES]
                cube[second, :] = got[:, LANES:]
            return carry

        lax.fori_loop(0, NG // many, one, 0)

    def along_x(step, carry):
        for u in range(0, many, 2):
            first, second = step * many + u, step * many + u + 1
            at = [pl.ds(m, NG, stride=NG) for m in (first, second)]
            both = jnp.concatenate([stack(cube[at[0], :]), stack(cube[at[1], :])], axis=1)
            got = dot(left_ref[0], both)
            got = [
                got[:, k * LANES : (k + 1) * LANES] * weights[pl.ds(pl.multiple_of(m * NG, NG), NG), :]
                for k, m in enumerate((first, second))
            ]
            got = dot(left_ref[1], jnp.concatenate([stack(got[0]), stack(got[1])], axis=1))
            cube[at[0], :] = got[:, :LANES]
            cube[at[1], :] = got[:, LANES:]
        return carry

    along_y(0)
    lax.fori_loop(0, NG // many, along_x, 0)
    along_y(1)
    tile = [None, None, None]
    for line in range(8):
        at = slice(line * LANES, (line + 1) * LANES)
        for i in range(rows):
            cells[i * N_GRID : (i + 1) * N_GRID, :] = cube[pl.ds(8 * i + line, N_GRID, stride=8 * rows), :]
        value = cells[...]
        high = value.astype(BF16)
        low = (value - high.astype(F32)).astype(BF16)
        for t in spans(line):
            lanes = slice(t * LANES, (t + 1) * LANES)
            term = dot_nt(high, zline[0, lanes, at]) + dot_nt(low, zline[0, lanes, at])
            term = term + dot_nt(high, zline[1, lanes, at])
            tile[t] = term if tile[t] is None else tile[t] + term
    for i in range(rows):
        for t in range(3):
            flat[pl.ds(row_of(3 * i + t), N_GRID, stride=SLOT), :] = tile[t][i * N_GRID : (i + 1) * N_GRID, :]
    send_b[...] = flat[...].reshape(N_GRID, SLOT, LANES).astype(BF16)

    own = pltpu.make_async_copy(send_b.at[grid], recv_b.at[grid], local)
    spreads = [spread(send_b, recv_b, b_s.at[p], b_r.at[p], first, past) for p, (first, past, _) in enumerate(pieces)]
    own.start()
    own.wait()
    sums = []
    for p, (first, past, span) in enumerate(pieces):
        for copy in spreads[p]:
            copy.wait_recv()
        flat[: N_GRID * PIECE, :] = recv_b[:, first : first + PIECE, :].astype(F32).reshape(N_GRID * PIECE, LANES)
        for i in span:
            at = slice(i * 384, (i + 1) * 384)
            got = [flat[pl.ds(row_of(3 * i + t) - first, group, stride=PIECE), :] for t in range(3)]
            weighted = (jnp.concatenate(got, axis=1) * density[:, at]).astype(BF16)
            y_out[:, :, at] = dot(ordered, weighted).astype(BF16).reshape(N_Y, targets_n // N_Y, 384)
        lanes = pl.ds(span[0] * 384, len(span) * 384)
        copies = [
            push(
                y_out.at[lax.rem(y + d, N_Y), :, lanes], y_in.at[d - 1, :, lanes],
                y_s.at[p, d - 1], y_r.at[p, d - 1], {"slab": y_peer(d)},
            )
            for d in range(1, N_Y)
        ]
        for copy in copies:
            copy.wait()
        for i in span:
            at = slice(i * 384, (i + 1) * 384)
            total = y_out[y, :, at].astype(F32)
            for d in range(N_Y - 1):
                total = total + y_in[d, :, at].astype(F32)
            for t in range(3):
                lo_flat[pl.ds(row_of(3 * i + t), N_LO * each, stride=SLOT), :] = total[:, t * LANES : (t + 1) * LANES]
        half = lo_flat[...].reshape(N_LO * each, SLOT, LANES)[:, first : first + PIECE, :].astype(BF16)
        lo_out[:, :, first : first + PIECE, :] = half.reshape(N_LO, each, PIECE, LANES)
        sums += [
            push(
                lo_out.at[lax.rem(lo + d, N_LO), :, pl.ds(first, past - first)],
                lo_in.at[d - 1, :, pl.ds(first, past - first)],
                lo_s.at[p, d - 1], lo_r.at[p, d - 1], {"slab": lo_peer(d)},
            )
            for d in range(1, N_LO)
        ]
    for copy in spreads[0] + spreads[1]:
        copy.wait_send()
    for copy in sums:
        copy.wait()
    total = lo_out[lo].astype(F32)
    for d in range(N_LO - 1):
        total = total + lo_in[d].astype(F32)
    last[...] = (total * (-1.0 / math.sqrt(group * N_LO * N_Y))).reshape(each * SLOT, LANES)
    for c in range(tiles):
        out_ref[:, c * LANES : (c + 1) * LANES] = last[pl.ds(row_of(c), each, stride=SLOT), :]


def body(orbitals, targets, points, fit):
    occupied, shard = orbitals.shape
    targets_n, group = targets.shape[0], points.shape[0]
    each = targets_n // (N_LO * N_Y)
    left, lines, square = tables()
    near, far = N_X * N_CORE - 1, N_HI - 1
    peers = N_GRID - 1
    dma = pltpu.SemaphoreType.DMA
    vmem = pltpu.VMEM
    return pl.pallas_call(
        functools.partial(kernel, occupied, targets_n, group, shard),
        out_shape=jax.ShapeDtypeStruct((each, shard), F32),
        in_specs=[pl.BlockSpec(memory_space=pl.ANY)] * 7,
        out_specs=pl.BlockSpec(memory_space=pltpu.VMEM),
        scratch_shapes=[
            vmem(orbitals.shape, BF16),
            vmem((1, targets_n), jnp.int32),
            vmem((1, group), jnp.int32),
            vmem(fit.shape, F32),
            vmem(left.shape, BF16),
            vmem(lines.shape, BF16),
            vmem(square.shape, F32),
            vmem((group, occupied), BF16),
            vmem((near, group, occupied), BF16),
            vmem((group, occupied), BF16),
            vmem((far, group, occupied), BF16),
            vmem((targets_n, shard), BF16),
            vmem((group, shard), F32),
            vmem((N_GRID * SLOT, LANES), F32),
            vmem((N_GRID * shard // 384, 384), BF16),
            vmem((N_GRID * shard // 384, LANES), F32),
            vmem((NG * NG, LANES), F32),
            vmem((NG * NG, LANES), F32),
            vmem((2, 384, 8 * LANES), BF16),
            vmem((N_GRID, SLOT, LANES), BF16),
            vmem((N_GRID, SLOT, LANES), BF16),
            vmem((N_GRID, SLOT, LANES), BF16),
            vmem((N_GRID, SLOT, LANES), BF16),
            vmem((N_Y, targets_n // N_Y, shard), BF16),
            vmem((N_Y - 1, targets_n // N_Y, shard), BF16),
            vmem((N_LO * each * SLOT, LANES), F32),
            vmem((N_LO, each, SLOT, LANES), BF16),
            vmem((N_LO - 1, each, SLOT, LANES), BF16),
            vmem((each * SLOT, LANES), F32),
            dma((near,)), dma((near,)), dma((far,)), dma((far,)),
            dma((peers,)), dma((peers,)), dma((2, peers)), dma((2, peers)),
            dma((2, N_Y - 1)), dma((2, N_Y - 1)), dma((2, N_LO - 1)), dma((2, N_LO - 1)), dma, dma((7,)),
        ],
        compiler_params=pltpu.CompilerParams(collective_id=0, has_side_effects=True, vmem_limit_bytes=60 * 1024 * 1024),
        name="exchange_operator",
    )(
        orbitals, targets.reshape(1, -1), points.reshape(1, -1), fit,
        jnp.asarray(left), jnp.asarray(lines), jnp.asarray(square),
    )


def solution(mesh):
    in_specs = (P(None, "grid"), P(), P("slab"), P("slab", None))
    out_specs = P("slab", "grid")
    return jax.shard_map(body, mesh=mesh, in_specs=in_specs, out_specs=out_specs, check_vma=False)
```

```python
import functools
import math

import jax
import jax.numpy as jnp
import numpy as np
from jax import lax
from jax.experimental import pallas as pl
from jax.experimental.pallas import tpu as pltpu
from jax.sharding import PartitionSpec as P

NG = 48
SCREENING = 4.0
MESH = pl.DeviceIdType.MESH
N_X, N_HI, N_CORE = 4, 4, 2
N_LO, N_Y = 8, 4
N_GRID = N_X * N_HI * N_CORE
LANES = 128
SLOT = 32
PIECE = 16
F32, BF16 = jnp.float32, jnp.bfloat16


def real_basis():
    rows, freq = [], []
    place = np.arange(NG)
    for m in range(NG // 2 + 1):
        scale = math.sqrt((1.0 if m in (0, NG // 2) else 2.0) / NG)
        rows.append(scale * np.cos(2.0 * math.pi * m * place / NG))
        freq.append(m)
    for m in range(1, NG // 2):
        rows.append(math.sqrt(2.0 / NG) * np.sin(2.0 * math.pi * m * place / NG))
        freq.append(m)
    return np.array(rows), np.array(freq)


def split_table(table):
    high = table.astype(BF16)
    low = (table - high.astype(np.float64)).astype(BF16)
    return high, low


def tables():
    basis, freq = real_basis()
    left = []
    for matrix in (basis, basis.T):
        high, low = split_table(matrix)
        left.append(np.concatenate([high, high, low], axis=1))
    lines = np.zeros((2 * NG, LANES), BF16)
    high, low = split_table(basis.T)
    lines[:NG, :NG] = high
    lines[NG:, :NG] = low
    square = ((2.0 * math.pi * freq / NG) ** 2).astype(np.float32)
    column = np.broadcast_to(square[:, None], (NG, LANES)).copy()
    row = np.zeros((8, LANES), np.float32)
    row[:, :NG] = square
    return np.stack(left), lines, np.concatenate([column, row])


def stack(values):
    high = values.astype(BF16)
    low = (values - high.astype(F32)).astype(BF16)
    return jnp.concatenate([high, low, high], axis=0)


def dot(a, b):
    return jnp.dot(a, b, preferred_element_type=F32)


def dot_nt(a, b):
    return lax.dot_general(a, b, (((1,), (1,)), ((), ())), preferred_element_type=F32)


def column_of(row, count):
    same = lax.broadcasted_iota(jnp.int32, (count, count), 0) == lax.broadcasted_iota(jnp.int32, (count, count), 1)
    return jnp.sum(jnp.where(same, row, 0), axis=1, keepdims=True)


def row_of(tile):
    return tile + (tile >= PIECE - 1)


def spans(line):
    return range(line * NG // LANES, (line * NG + NG - 1) // LANES + 1)


def kernel(
    occupied, targets_n, group, shard, orb_hbm, targets_hbm, points_hbm, fit_hbm, left_hbm, lines_hbm, square_hbm,
    out_ref, orb_ref, targets_ref, points_ref, fit_ref, left_ref, lines_ref, square_ref, mine, near, part, far, chosen, density, flat, packed, cells, cube, weights, zline,
    send_a, recv_a, send_b, recv_b, y_out, y_in, lo_flat, lo_out, lo_in, last,
    near_s, near_r, far_s, far_r, a_s, a_r, b_s, b_r, y_s, y_r, lo_s, lo_r, local, fetched,
):
    grid, slab = lax.axis_index("grid"), lax.axis_index("slab")
    core, hi, x = lax.rem(grid, N_CORE), lax.rem(grid // N_CORE, N_HI), grid // (N_CORE * N_HI)
    lo, y = slab // N_Y, lax.rem(slab, N_Y)
    tiles = shard // LANES
    rows = tiles // 3
    wire = row_of(tiles - 1) + 1
    pieces = [(0, PIECE, range((PIECE - 1) // 3)), (PIECE, wire, range((PIECE - 1) // 3, rows))]
    each = targets_n // (N_LO * N_Y)

    def grid_peer(dx, dh, dc):
        return (lax.rem(x + dx, N_X) * N_HI + lax.rem(hi + dh, N_HI)) * N_CORE + lax.rem(core + dc, N_CORE)

    def y_peer(d):
        return lo * N_Y + lax.rem(y + d, N_Y)

    def lo_peer(d):
        return lax.rem(lo + d, N_LO) * N_Y + y

    offsets = [(dx, dh, dc) for hs in ((2,), (1, 3), (0,)) for dx in (2, 1, 3, 0) for dc in (1, 0) for dh in hs if dx or dh or dc]
    fetches = [
        pltpu.make_async_copy(source, target, fetched.at[i])
        for i, (source, target) in enumerate(
            [
                (points_hbm, points_ref), (orb_hbm, orb_ref), (targets_hbm, targets_ref), (lines_hbm, lines_ref),
                (square_hbm, square_ref), (fit_hbm, fit_ref), (left_hbm, left_ref),
            ]
        )
    ]
    barrier = pltpu.get_barrier_semaphore()
    for step in offsets:
        pl.semaphore_signal(barrier, inc=1, device_id={"grid": grid_peer(*step)}, device_id_type=MESH)
    for d in range(1, N_Y):
        pl.semaphore_signal(barrier, inc=1, device_id={"slab": y_peer(d)}, device_id_type=MESH)
    for d in range(1, N_LO):
        pl.semaphore_signal(barrier, inc=1, device_id={"slab": lo_peer(d)}, device_id_type=MESH)

    for fetch in fetches:
        fetch.start()

    def push(src, dst, send, recv, peer):
        copy = pltpu.make_async_remote_copy(
            src_ref=src, dst_ref=dst, send_sem=send, recv_sem=recv, device_id=peer, device_id_type=MESH
        )
        copy.start()
        return copy

    flat[...] = jnp.zeros_like(flat)
    lo_flat[...] = jnp.zeros_like(lo_flat)
    zline[...] = jnp.zeros_like(zline)
    for fetch in fetches:
        fetch.wait()
    offset = column_of(points_ref[...], group) - grid * shard
    for i in range(rows):
        ids = lax.broadcasted_iota(jnp.int32, (group, 384), 1) + i * 384
        term = dot_nt(
            jnp.where(ids == offset, 1.0, 0.0).astype(BF16), orb_ref[:, i * 384 : (i + 1) * 384]
        )
        total = term if i == 0 else total + term
    mine[...] = total.astype(BF16)
    targets = targets_ref[...]
    occ = lax.broadcasted_iota(jnp.int32, (occupied, targets_n), 0)
    choose = jnp.where(occ == targets, 1.0, 0.0).astype(BF16)
    pick = jnp.where(
        lax.broadcasted_iota(jnp.int32, (targets_n, occupied), 1) == column_of(targets, targets_n), 1.0, 0.0
    ).astype(BF16)
    new = lax.broadcasted_iota(jnp.int32, (targets_n, targets_n), 0)
    old = lax.broadcasted_iota(jnp.int32, (targets_n, targets_n), 1)
    from_old = ((new // each) % N_LO) * (N_Y * each) + (new // (each * N_LO)) * each + new % each
    reorder = dot(jnp.where(old == from_old, 1.0, 0.0).astype(BF16), pick).astype(BF16)
    for i in range(rows):
        chosen[:, i * 384 : (i + 1) * 384] = dot(pick, orb_ref[:, i * 384 : (i + 1) * 384]).astype(BF16)
    for line in range(8):
        at = slice(line * NG, (line + 1) * NG)
        for k in range(2):
            zline[k, at, line * LANES : (line + 1) * LANES] = lines_ref[k * NG : (k + 1) * NG, :]
    column, row = square_ref[:NG, :], square_ref[NG : NG + 1, :]

    def weigh(m, carry):
        one = square_ref[pl.ds(m, 1), :]
        weights[pl.ds(pl.multiple_of(m * NG, NG), NG), :] = SCREENING / (SCREENING + column + row + one[:, :1])
        return carry

    lax.fori_loop(0, NG, weigh, 0)
    fit = fit_ref[...]
    fit_1 = fit.astype(BF16)
    fit_2 = (fit - fit_1.astype(F32)).astype(BF16)
    fit_3 = (fit - fit_1.astype(F32) - fit_2.astype(F32)).astype(BF16)
    fits = jnp.concatenate([fit_1, fit_1, fit_2, fit_1, fit_2, fit_3], axis=1)

    pl.semaphore_wait(barrier, len(offsets) + N_Y - 1 + N_LO - 1)

    near_steps = [(dx, 0, dc) for dx in range(N_X) for dc in range(N_CORE) if dx or dc]
    copies = [
        push(mine, near.at[i], near_s.at[i], near_r.at[i], {"grid": grid_peer(*step)})
        for i, step in enumerate(near_steps)
    ]
    for copy in copies:
        copy.wait()
    total = mine[...].astype(F32)
    for i in range(len(near_steps)):
        total = total + near[i].astype(F32)
    part[...] = total.astype(BF16)
    copies = [
        push(part, far.at[d - 1], far_s.at[d - 1], far_r.at[d - 1], {"grid": grid_peer(0, d, 0)})
        for d in range(1, N_HI)
    ]
    for copy in copies:
        copy.wait()
    for i in range(N_HI - 1):
        total = total + far[i].astype(F32)
    at_points = total.astype(BF16)

    target_points = dot(at_points, choose).astype(BF16)
    ordered = dot_nt(reorder, at_points).astype(BF16)
    for i in range(rows):
        at = slice(i * 384, (i + 1) * 384)
        dense = dot(at_points, orb_ref[:, at]) * (1.0 / math.sqrt(occupied))
        density[:, at] = dense
        pair = dense * (dot(target_points, chosen[:, at]) * (1.0 / math.sqrt(targets_n)))
        pair_1 = pair.astype(BF16)
        rest = pair - pair_1.astype(F32)
        pair_2 = rest.astype(BF16)
        pair_3 = (rest - pair_2.astype(F32)).astype(BF16)
        fitted = dot(fits, jnp.concatenate([pair_1, pair_2, pair_1, pair_3, pair_2, pair_1], axis=0))
        for t in range(3):
            flat[pl.ds(row_of(3 * i + t), group, stride=SLOT), :] = fitted[:, t * LANES : (t + 1) * LANES]
    send_a[...] = flat[...].reshape(N_GRID, SLOT, LANES).astype(BF16)

    def spread(source, target, send, recv, first, past):
        copies = []
        for i, step in enumerate(offsets):
            peer = grid_peer(*step)
            copies.append(
                push(
                    source.at[peer, pl.ds(first, past - first)], target.at[grid, pl.ds(first, past - first)],
                    send.at[i], recv.at[i], {"grid": peer},
                )
            )
        return copies

    own = pltpu.make_async_copy(send_a.at[grid], recv_a.at[grid], local)
    copies = spread(send_a, recv_a, a_s, a_r, 0, wire)
    own.start()
    own.wait()
    for copy in copies:
        copy.wait()
    flat[...] = recv_a[...].astype(F32).reshape(N_GRID * SLOT, LANES)

    for i in range(rows):
        for t in range(3):
            packed[i * N_GRID : (i + 1) * N_GRID, t * LANES : (t + 1) * LANES] = flat[
                pl.ds(row_of(3 * i + t), N_GRID, stride=SLOT), :
            ].astype(BF16)
    for line in range(8):
        at = slice(line * LANES, (line + 1) * LANES)
        got = None
        for t in spans(line):
            lanes = slice(t * LANES, (t + 1) * LANES)
            for k in range(2):
                term = dot(packed[:, lanes], zline[k, lanes, at])
                got = term if got is None else got + term
        for i in range(rows):
            cube[pl.ds(8 * i + line, N_GRID, stride=8 * rows), :] = got[i * N_GRID : (i + 1) * N_GRID, :]

    many = 8

    def pairs_of(values):
        return [jnp.concatenate([stack(a), stack(b)], axis=1) for a, b in zip(values[::2], values[1::2])]

    def apart(values):
        return [v[:, k * LANES : (k + 1) * LANES] for v in values for k in range(2)]

    def along_y(which):
        def one(step, carry):
            at = [pl.ds(pl.multiple_of((step * many + u) * NG, NG), NG) for u in range(many)]
            left = left_ref[which]
            got = apart([dot(left, both) for both in pairs_of([cube[a, :] for a in at])])
            for a, value in zip(at, got):
                cube[a, :] = value
            return carry

        lax.fori_loop(0, NG // many, one, 0)

    def along_x(step, carry):
        at = [pl.ds(step * many + u, NG, stride=NG) for u in range(many)]
        scale = [pl.ds(pl.multiple_of((step * many + u) * NG, NG), NG) for u in range(many)]
        left, back = left_ref[0], left_ref[1]
        got = apart([dot(left, both) for both in pairs_of([cube[a, :] for a in at])])
        got = [value * weights[m, :] for value, m in zip(got, scale)]
        got = apart([dot(back, both) for both in pairs_of(got)])
        for a, value in zip(at, got):
            cube[a, :] = value
        return carry

    along_y(0)
    lax.fori_loop(0, NG // many, along_x, 0)
    along_y(1)
    tile = [None, None, None]
    for line in range(8):
        at = slice(line * LANES, (line + 1) * LANES)
        for i in range(rows):
            cells[i * N_GRID : (i + 1) * N_GRID, :] = cube[pl.ds(8 * i + line, N_GRID, stride=8 * rows), :]
        value = cells[...]
        high = value.astype(BF16)
        low = (value - high.astype(F32)).astype(BF16)
        for t in spans(line):
            lanes = slice(t * LANES, (t + 1) * LANES)
            term = dot_nt(high, zline[0, lanes, at]) + dot_nt(low, zline[0, lanes, at])
            term = term + dot_nt(high, zline[1, lanes, at])
            tile[t] = term if tile[t] is None else tile[t] + term
    for i in range(rows):
        for t in range(3):
            flat[pl.ds(row_of(3 * i + t), N_GRID, stride=SLOT), :] = tile[t][i * N_GRID : (i + 1) * N_GRID, :]
    send_b[...] = flat[...].reshape(N_GRID, SLOT, LANES).astype(BF16)

    own = pltpu.make_async_copy(send_b.at[grid], recv_b.at[grid], local)
    spreads = [spread(send_b, recv_b, b_s.at[p], b_r.at[p], first, past) for p, (first, past, _) in enumerate(pieces)]
    own.start()
    own.wait()
    sums = []
    for p, (first, past, span) in enumerate(pieces):
        for copy in spreads[p]:
            copy.wait_recv()
        flat[: N_GRID * PIECE, :] = recv_b[:, first : first + PIECE, :].astype(F32).reshape(N_GRID * PIECE, LANES)
        for i in span:
            at = slice(i * 384, (i + 1) * 384)
            got = [flat[pl.ds(row_of(3 * i + t) - first, group, stride=PIECE), :] for t in range(3)]
            weighted = (jnp.concatenate(got, axis=1) * density[:, at]).astype(BF16)
            y_out[:, :, at] = dot(ordered, weighted).astype(BF16).reshape(N_Y, targets_n // N_Y, 384)
        lanes = pl.ds(span[0] * 384, len(span) * 384)
        copies = [
            push(
                y_out.at[lax.rem(y + d, N_Y), :, lanes], y_in.at[d - 1, :, lanes],
                y_s.at[p, d - 1], y_r.at[p, d - 1], {"slab": y_peer(d)},
            )
            for d in range(1, N_Y)
        ]
        for copy in copies:
            copy.wait()
        for i in span:
            at = slice(i * 384, (i + 1) * 384)
            total = y_out[y, :, at].astype(F32)
            for d in range(N_Y - 1):
                total = total + y_in[d, :, at].astype(F32)
            for t in range(3):
                lo_flat[pl.ds(row_of(3 * i + t), N_LO * each, stride=SLOT), :] = total[:, t * LANES : (t + 1) * LANES]
        half = lo_flat[...].reshape(N_LO * each, SLOT, LANES)[:, first : first + PIECE, :].astype(BF16)
        lo_out[:, :, first : first + PIECE, :] = half.reshape(N_LO, each, PIECE, LANES)
        sums += [
            push(
                lo_out.at[lax.rem(lo + d, N_LO), :, pl.ds(first, past - first)],
                lo_in.at[d - 1, :, pl.ds(first, past - first)],
                lo_s.at[p, d - 1], lo_r.at[p, d - 1], {"slab": lo_peer(d)},
            )
            for d in range(1, N_LO)
        ]
    for copy in spreads[0] + spreads[1]:
        copy.wait_send()
    for copy in sums:
        copy.wait()
    total = lo_out[lo].astype(F32)
    for d in range(N_LO - 1):
        total = total + lo_in[d].astype(F32)
    last[...] = (total * (-1.0 / math.sqrt(group * N_LO * N_Y))).reshape(each * SLOT, LANES)
    for c in range(tiles):
        out_ref[:, c * LANES : (c + 1) * LANES] = last[pl.ds(row_of(c), each, stride=SLOT), :]


def body(orbitals, targets, points, fit):
    occupied, shard = orbitals.shape
    targets_n, group = targets.shape[0], points.shape[0]
    each = targets_n // (N_LO * N_Y)
    left, lines, square = tables()
    near, far = N_X * N_CORE - 1, N_HI - 1
    peers = N_GRID - 1
    dma = pltpu.SemaphoreType.DMA
    vmem = pltpu.VMEM
    return pl.pallas_call(
        functools.partial(kernel, occupied, targets_n, group, shard),
        out_shape=jax.ShapeDtypeStruct((each, shard), F32),
        in_specs=[pl.BlockSpec(memory_space=pl.ANY)] * 7,
        out_specs=pl.BlockSpec(memory_space=pltpu.VMEM),
        scratch_shapes=[
            vmem(orbitals.shape, BF16),
            vmem((1, targets_n), jnp.int32),
            vmem((1, group), jnp.int32),
            vmem(fit.shape, F32),
            vmem(left.shape, BF16),
            vmem(lines.shape, BF16),
            vmem(square.shape, F32),
            vmem((group, occupied), BF16),
            vmem((near, group, occupied), BF16),
            vmem((group, occupied), BF16),
            vmem((far, group, occupied), BF16),
            vmem((targets_n, shard), BF16),
            vmem((group, shard), F32),
            vmem((N_GRID * SLOT, LANES), F32),
            vmem((N_GRID * shard // 384, 384), BF16),
            vmem((N_GRID * shard // 384, LANES), F32),
            vmem((NG * NG, LANES), F32),
            vmem((NG * NG, LANES), F32),
            vmem((2, 384, 8 * LANES), BF16),
            vmem((N_GRID, SLOT, LANES), BF16),
            vmem((N_GRID, SLOT, LANES), BF16),
            vmem((N_GRID, SLOT, LANES), BF16),
            vmem((N_GRID, SLOT, LANES), BF16),
            vmem((N_Y, targets_n // N_Y, shard), BF16),
            vmem((N_Y - 1, targets_n // N_Y, shard), BF16),
            vmem((N_LO * each * SLOT, LANES), F32),
            vmem((N_LO, each, SLOT, LANES), BF16),
            vmem((N_LO - 1, each, SLOT, LANES), BF16),
            vmem((each * SLOT, LANES), F32),
            dma((near,)), dma((near,)), dma((far,)), dma((far,)),
            dma((peers,)), dma((peers,)), dma((2, peers)), dma((2, peers)),
            dma((2, N_Y - 1)), dma((2, N_Y - 1)), dma((2, N_LO - 1)), dma((2, N_LO - 1)), dma, dma((7,)),
        ],
        compiler_params=pltpu.CompilerParams(collective_id=0, has_side_effects=True, vmem_limit_bytes=60 * 1024 * 1024),
        name="exchange_operator",
    )(
        orbitals, targets.reshape(1, -1), points.reshape(1, -1), fit,
        jnp.asarray(left), jnp.asarray(lines), jnp.asarray(square),
    )


def solution(mesh):
    in_specs = (P(None, "grid"), P(), P("slab"), P("slab", None))
    out_specs = P("slab", "grid")
    return jax.shard_map(body, mesh=mesh, in_specs=in_specs, out_specs=out_specs, check_vma=False)
```

```python
import functools
import math

import jax
import jax.numpy as jnp
import numpy as np
from jax import lax
from jax.experimental import pallas as pl
from jax.experimental.pallas import tpu as pltpu
from jax.sharding import PartitionSpec as P

NG = 48
SCREENING = 4.0
MESH = pl.DeviceIdType.MESH
N_X, N_HI, N_CORE = 4, 4, 2
N_LO, N_Y = 8, 4
N_GRID = N_X * N_HI * N_CORE
LANES = 128
SLOT = 32
PIECE = 16
F32, BF16 = jnp.float32, jnp.bfloat16


def real_basis():
    rows, freq = [], []
    place = np.arange(NG)
    for m in range(NG // 2 + 1):
        scale = math.sqrt((1.0 if m in (0, NG // 2) else 2.0) / NG)
        rows.append(scale * np.cos(2.0 * math.pi * m * place / NG))
        freq.append(m)
    for m in range(1, NG // 2):
        rows.append(math.sqrt(2.0 / NG) * np.sin(2.0 * math.pi * m * place / NG))
        freq.append(m)
    return np.array(rows), np.array(freq)


def split_table(table):
    high = table.astype(BF16)
    low = (table - high.astype(np.float64)).astype(BF16)
    return high, low


def tables():
    basis, freq = real_basis()
    left = []
    for matrix in (basis, basis.T):
        high, low = split_table(matrix)
        left.append(np.concatenate([high, high, low], axis=1))
    lines = np.zeros((2 * NG, LANES), BF16)
    high, low = split_table(basis.T)
    lines[:NG, :NG] = high
    lines[NG:, :NG] = low
    square = ((2.0 * math.pi * freq / NG) ** 2).astype(np.float32)
    column = np.broadcast_to(square[:, None], (NG, LANES)).copy()
    row = np.zeros((8, LANES), np.float32)
    row[:, :NG] = square
    return np.stack(left), lines, np.concatenate([column, row])


def stack(values):
    high = values.astype(BF16)
    low = (values - high.astype(F32)).astype(BF16)
    return jnp.concatenate([high, low, high], axis=0)


def dot(a, b):
    return jnp.dot(a, b, preferred_element_type=F32)


def dot_nt(a, b):
    return lax.dot_general(a, b, (((1,), (1,)), ((), ())), preferred_element_type=F32)


def column_of(row, count):
    same = lax.broadcasted_iota(jnp.int32, (count, count), 0) == lax.broadcasted_iota(jnp.int32, (count, count), 1)
    return jnp.sum(jnp.where(same, row, 0), axis=1, keepdims=True)


def row_of(tile):
    return tile + (tile >= PIECE - 1)


def spans(line):
    return range(line * NG // LANES, (line * NG + NG - 1) // LANES + 1)


def kernel(
    occupied, targets_n, group, shard, orb_hbm, targets_hbm, points_hbm, fit_hbm, left_hbm, lines_hbm, square_hbm,
    out_ref, orb_ref, targets_ref, points_ref, fit_ref, left_ref, lines_ref, square_ref, mine, near, part, far, home_at, task_at, task_fit, task_orb, density, flat, packed, cells, cube, weights, zline,
    send_a, recv_a, send_b, recv_b, y_out, y_in, lo_flat, lo_out, lo_in, last,
    near_s, near_r, far_s, far_r, orb_s, orb_r, all_s, all_r, at_s, at_r, fit_s, fit_r, a_s, a_r, b_s, b_r, y_s, y_r, lo_s, lo_r, local, fetched,
):
    grid, slab = lax.axis_index("grid"), lax.axis_index("slab")
    core, hi, x = lax.rem(grid, N_CORE), lax.rem(grid // N_CORE, N_HI), grid // (N_CORE * N_HI)
    lo, y = slab // N_Y, lax.rem(slab, N_Y)
    tiles = shard // LANES
    rows = tiles // 3
    wire = row_of(tiles - 1) + 1
    pieces = [(0, PIECE, range((PIECE - 1) // 3)), (PIECE, wire, range((PIECE - 1) // 3, rows))]
    each = targets_n // (N_LO * N_Y)

    half, place = lo // N_HI, lax.rem(lo, N_HI)
    at_home = place == hi
    quarter = occupied // N_Y

    def grid_peer(dx, dh, dc):
        return (lax.rem(x + dx, N_X) * N_HI + lax.rem(hi + dh, N_HI)) * N_CORE + lax.rem(core + dc, N_CORE)

    def place_slab(where):
        return (half * N_HI + where) * N_Y + y

    def task_peer(dx, dp, dc):
        return {"grid": grid_peer(dx, 0, dc), "slab": place_slab(lax.rem(place + dp, N_HI))}

    def vector_of(dx, dp, dc):
        return (lax.rem(x + dx, N_X) * N_HI + lax.rem(place + dp, N_HI)) * N_CORE + lax.rem(core + dc, N_CORE)

    vector = vector_of(0, 0, 0)

    def block_of(dx, dp, dc):
        return (lax.rem(x + dx, N_X) * N_HI + lax.rem(place + dp + hi, N_HI)) * N_CORE + lax.rem(core + dc, N_CORE)

    block = block_of(0, 0, 0)
    away = place != 0

    def cells_peer(d):
        return {"grid": grid_peer(0, place, 0), "slab": lax.rem(lo + d, N_LO) * N_Y + y}

    def source_peer(dh, da):
        where = lax.rem(half + da, N_LO // N_HI) * N_HI + lax.rem(N_HI + N_HI - dh, N_HI)
        return {"grid": grid_peer(0, dh, 0), "slab": where * N_Y + y}

    def y_peer(d):
        return lo * N_Y + lax.rem(y + d, N_Y)

    def steps(order):
        return [(dx, d, dc) for ds in order for dx in (2, 1, 3, 0) for dc in (1, 0) for d in ds]

    tasks = [step for step in steps(((2,), (1, 3), (0,))) if any(step)]
    sources = [(dh, da) for dh in range(N_HI) for da in range(N_LO // N_HI)]
    fetches = [
        pltpu.make_async_copy(source, target, fetched.at[i])
        for i, (source, target) in enumerate(
            [
                (points_hbm, points_ref), (orb_hbm, orb_ref), (targets_hbm, targets_ref), (lines_hbm, lines_ref),
                (square_hbm, square_ref), (fit_hbm, fit_ref), (left_hbm, left_ref),
            ]
        )
    ]
    barrier = pltpu.get_barrier_semaphore()

    def hello(peer):
        pl.semaphore_signal(barrier, inc=1, device_id=peer, device_id_type=MESH)

    for d in range(1, N_HI):
        hello({"grid": grid_peer(0, d, 0)})
    for step in sources:
        if any(step):
            hello(source_peer(*step))
    pl.when(away)(lambda: hello(source_peer(0, 0)))
    for step in tasks:
        hello(task_peer(*step))
    for d in range(1, N_Y):
        pl.semaphore_signal(barrier, inc=1, device_id={"slab": y_peer(d)}, device_id_type=MESH)
    for fetch in fetches:
        fetch.start()

    def push(src, dst, send, recv, peer):
        copy = pltpu.make_async_remote_copy(
            src_ref=src, dst_ref=dst, send_sem=send, recv_sem=recv, device_id=peer, device_id_type=MESH
        )
        copy.start()
        return copy

    flat[...] = jnp.zeros_like(flat)
    lo_flat[...] = jnp.zeros_like(lo_flat)
    zline[...] = jnp.zeros_like(zline)
    for fetch in fetches:
        fetch.wait()
    offset = column_of(points_ref[...], group) - grid * shard
    for i in range(rows):
        ids = lax.broadcasted_iota(jnp.int32, (group, 384), 1) + i * 384
        term = dot_nt(
            jnp.where(ids == offset, 1.0, 0.0).astype(BF16), orb_ref[:, i * 384 : (i + 1) * 384]
        )
        total = term if i == 0 else total + term
    mine[...] = total.astype(BF16)
    targets = targets_ref[...]
    occ = lax.broadcasted_iota(jnp.int32, (occupied, targets_n), 0)
    choose = jnp.where(occ == targets, 1.0, 0.0).astype(BF16)
    pick = jnp.where(
        lax.broadcasted_iota(jnp.int32, (targets_n, occupied), 1) == column_of(targets, targets_n), 1.0, 0.0
    ).astype(BF16)
    new = lax.broadcasted_iota(jnp.int32, (targets_n, targets_n), 0)
    old = lax.broadcasted_iota(jnp.int32, (targets_n, targets_n), 1)
    from_old = ((new // each) % N_LO) * (N_Y * each) + (new // (each * N_LO)) * each + new % each
    reorder = dot(jnp.where(old == from_old, 1.0, 0.0).astype(BF16), pick).astype(BF16)
    for line in range(8):
        at = slice(line * NG, (line + 1) * NG)
        for k in range(2):
            zline[k, at, line * LANES : (line + 1) * LANES] = lines_ref[k * NG : (k + 1) * NG, :]
    column, row = square_ref[:NG, :], square_ref[NG : NG + 1, :]

    def weigh(m, carry):
        one = square_ref[pl.ds(m, 1), :]
        weights[pl.ds(pl.multiple_of(m * NG, NG), NG), :] = SCREENING / (SCREENING + column + row + one[:, :1])
        return carry

    lax.fori_loop(0, NG, weigh, 0)
    greetings = N_HI - 1 + len(tasks) + N_LO - 1 + N_Y - 1
    pl.semaphore_wait(barrier, greetings + jnp.where(away, 1, 0))

    own_rows = pl.ds(pl.multiple_of(y * quarter, quarter), quarter)
    fetch_orb = pltpu.make_async_remote_copy(
        src_ref=orb_ref.at[own_rows], dst_ref=task_orb.at[own_rows], send_sem=orb_s, recv_sem=orb_r,
        device_id={"grid": grid_peer(0, N_HI - place, 0)}, device_id_type=MESH,
    )
    keep_orb = pltpu.make_async_copy(orb_ref.at[own_rows], task_orb.at[own_rows], orb_r)
    pl.when(away)(fetch_orb.start)
    pl.when(jnp.logical_not(away))(keep_orb.start)

    near_steps = [(dx, 0, dc) for dx in range(N_X) for dc in range(N_CORE) if dx or dc]
    copies = [
        push(mine, near.at[i], near_s.at[i], near_r.at[i], {"grid": grid_peer(*step)})
        for i, step in enumerate(near_steps)
    ]
    for copy in copies:
        copy.wait()
    total = mine[...].astype(F32)
    for i in range(len(near_steps)):
        total = total + near[i].astype(F32)
    part[...] = total.astype(BF16)
    copies = [
        push(part, far.at[d - 1], far_s.at[d - 1], far_r.at[d - 1], {"grid": grid_peer(0, d, 0)})
        for d in range(1, N_HI)
    ]
    for copy in copies:
        copy.wait()
    for i in range(N_HI - 1):
        total = total + far[i].astype(F32)
    at_points = total.astype(BF16)
    home_at[...] = at_points

    def hand(source, target, send, recv):
        return [
            pltpu.make_async_remote_copy(
                src_ref=source, dst_ref=target, send_sem=send.at[d - 1], recv_sem=recv,
                device_id=task_peer(0, d, 0), device_id_type=MESH,
            )
            for d in range(1, N_HI)
        ]

    hands = hand(home_at, task_at, at_s, at_r) + hand(fit_ref, task_fit, fit_s, fit_r)

    @pl.when(at_home)
    def _():
        for copy in hands:
            copy.start()
        task_at[...] = home_at[...]
        task_fit[...] = fit_ref[...]

    fetch_orb.wait_recv()
    copies = [
        push(task_orb.at[own_rows], task_orb.at[own_rows], all_s.at[d - 1], all_r.at[d - 1], {"slab": y_peer(d)})
        for d in range(1, N_Y)
    ]
    @pl.when(jnp.logical_not(at_home))
    def _():
        hands[0].wait_recv()
        hands[-1].wait_recv()

    at_task = task_at[...]
    ordered = dot_nt(reorder, at_task).astype(BF16)
    fit = task_fit[...]
    fit_1 = fit.astype(BF16)
    fit_2 = (fit - fit_1.astype(F32)).astype(BF16)
    fit_3 = (fit - fit_1.astype(F32) - fit_2.astype(F32)).astype(BF16)
    fits = jnp.concatenate([fit_1, fit_1, fit_2, fit_1, fit_2, fit_3], axis=1)
    target_points = dot(at_task, choose).astype(BF16)
    for d, copy in enumerate(copies):
        copy.wait_send()
    for d in range(1, N_Y):
        their_rows = pl.ds(pl.multiple_of(lax.rem(y + N_Y - d, N_Y) * quarter, quarter), quarter)
        pltpu.make_async_remote_copy(
            src_ref=task_orb.at[their_rows], dst_ref=task_orb.at[their_rows], send_sem=all_s.at[d - 1],
            recv_sem=all_r.at[d - 1], device_id={"slab": y_peer(d)}, device_id_type=MESH,
        ).wait_recv()
    for i in range(rows):
        at = slice(i * 384, (i + 1) * 384)
        orb = task_orb[:, at]
        dense = dot(at_task, orb) * (1.0 / math.sqrt(occupied))
        density[:, at] = dense
        chosen = dot(pick, orb).astype(BF16)
        pair = dense * (dot(target_points, chosen) * (1.0 / math.sqrt(targets_n)))
        pair_1 = pair.astype(BF16)
        rest = pair - pair_1.astype(F32)
        pair_2 = rest.astype(BF16)
        pair_3 = (rest - pair_2.astype(F32)).astype(BF16)
        fitted = dot(fits, jnp.concatenate([pair_1, pair_2, pair_1, pair_3, pair_2, pair_1], axis=0))
        for t in range(3):
            flat[pl.ds(row_of(3 * i + t), group, stride=SLOT), :] = fitted[:, t * LANES : (t + 1) * LANES]
    send_a[...] = flat[...].reshape(N_GRID, SLOT, LANES).astype(BF16)

    copies = [
        push(
            send_a.at[vector_of(*step), pl.ds(0, wire)], recv_a.at[block, pl.ds(0, wire)],
            a_s.at[i], a_r.at[i], task_peer(*step),
        )
        for i, step in enumerate(tasks)
    ]
    own = pltpu.make_async_copy(send_a.at[vector], recv_a.at[block], local)
    own.start()
    own.wait()
    for copy in copies:
        copy.wait()

    @pl.when(away)
    def _():
        fetch_orb.wait_send()

    @pl.when(at_home)
    def _():
        for copy in hands:
            copy.wait_send()

    flat[...] = recv_a[...].astype(F32).reshape(N_GRID * SLOT, LANES)

    for i in range(rows):
        for t in range(3):
            packed[i * N_GRID : (i + 1) * N_GRID, t * LANES : (t + 1) * LANES] = flat[
                pl.ds(row_of(3 * i + t), N_GRID, stride=SLOT), :
            ].astype(BF16)
    for line in range(8):
        at = slice(line * LANES, (line + 1) * LANES)
        got = None
        for t in spans(line):
            lanes = slice(t * LANES, (t + 1) * LANES)
            for k in range(2):
                term = dot(packed[:, lanes], zline[k, lanes, at])
                got = term if got is None else got + term
        for i in range(rows):
            cube[pl.ds(8 * i + line, N_GRID, stride=8 * rows), :] = got[i * N_GRID : (i + 1) * N_GRID, :]

    many = 8

    def pairs_of(values):
        return [jnp.concatenate([stack(a), stack(b)], axis=1) for a, b in zip(values[::2], values[1::2])]

    def apart(values):
        return [v[:, k * LANES : (k + 1) * LANES] for v in values for k in range(2)]

    def along_y(which):
        def one(step, carry):
            at = [pl.ds(pl.multiple_of((step * many + u) * NG, NG), NG) for u in range(many)]
            left = left_ref[which]
            got = apart([dot(left, both) for both in pairs_of([cube[a, :] for a in at])])
            for a, value in zip(at, got):
                cube[a, :] = value
            return carry

        lax.fori_loop(0, NG // many, one, 0)

    def along_x(step, carry):
        at = [pl.ds(step * many + u, NG, stride=NG) for u in range(many)]
        scale = [pl.ds(pl.multiple_of((step * many + u) * NG, NG), NG) for u in range(many)]
        left, back = left_ref[0], left_ref[1]
        got = apart([dot(left, both) for both in pairs_of([cube[a, :] for a in at])])
        got = [value * weights[m, :] for value, m in zip(got, scale)]
        got = apart([dot(back, both) for both in pairs_of(got)])
        for a, value in zip(at, got):
            cube[a, :] = value
        return carry

    along_y(0)
    lax.fori_loop(0, NG // many, along_x, 0)
    along_y(1)
    tile = [None, None, None]
    for line in range(8):
        at = slice(line * LANES, (line + 1) * LANES)
        for i in range(rows):
            cells[i * N_GRID : (i + 1) * N_GRID, :] = cube[pl.ds(8 * i + line, N_GRID, stride=8 * rows), :]
        value = cells[...]
        high = value.astype(BF16)
        low = (value - high.astype(F32)).astype(BF16)
        for t in spans(line):
            lanes = slice(t * LANES, (t + 1) * LANES)
            term = dot_nt(high, zline[0, lanes, at]) + dot_nt(low, zline[0, lanes, at])
            term = term + dot_nt(high, zline[1, lanes, at])
            tile[t] = term if tile[t] is None else tile[t] + term
    for i in range(rows):
        for t in range(3):
            flat[pl.ds(row_of(3 * i + t), N_GRID, stride=SLOT), :] = tile[t][i * N_GRID : (i + 1) * N_GRID, :]
    send_b[...] = flat[...].reshape(N_GRID, SLOT, LANES).astype(BF16)

    spreads = [
        [
            push(
                send_b.at[block_of(*step), pl.ds(first, past - first)],
                recv_b.at[vector, pl.ds(first, past - first)], b_s.at[p, i], b_r.at[p, i], task_peer(*step),
            )
            for i, step in enumerate(tasks)
        ]
        for p, (first, past, _) in enumerate(pieces)
    ]
    own = pltpu.make_async_copy(send_b.at[block], recv_b.at[vector], local)
    own.start()
    own.wait()
    sums = []
    sender = hi * (N_LO // N_HI) + half
    for p, (first, past, span) in enumerate(pieces):
        for copy in spreads[p]:
            copy.wait_recv()
        flat[: N_GRID * PIECE, :] = recv_b[:, first : first + PIECE, :].astype(F32).reshape(N_GRID * PIECE, LANES)
        for i in span:
            at = slice(i * 384, (i + 1) * 384)
            got = [flat[pl.ds(row_of(3 * i + t) - first, group, stride=PIECE), :] for t in range(3)]
            weighted = (jnp.concatenate(got, axis=1) * density[:, at]).astype(BF16)
            y_out[:, :, at] = dot(ordered, weighted).astype(BF16).reshape(N_Y, targets_n // N_Y, 384)
        lanes = pl.ds(span[0] * 384, len(span) * 384)
        copies = [
            push(
                y_out.at[lax.rem(y + d, N_Y), :, lanes], y_in.at[d - 1, :, lanes],
                y_s.at[p, d - 1], y_r.at[p, d - 1], {"slab": y_peer(d)},
            )
            for d in range(1, N_Y)
        ]
        for copy in copies:
            copy.wait()
        for i in span:
            at = slice(i * 384, (i + 1) * 384)
            total = y_out[y, :, at].astype(F32)
            for d in range(N_Y - 1):
                total = total + y_in[d, :, at].astype(F32)
            for t in range(3):
                lo_flat[pl.ds(row_of(3 * i + t), N_LO * each, stride=SLOT), :] = total[:, t * LANES : (t + 1) * LANES]
        piece = lo_flat[...].reshape(N_LO * each, SLOT, LANES)[:, first : first + PIECE, :].astype(BF16)
        lo_out[:, :, first : first + PIECE, :] = piece.reshape(N_LO, each, PIECE, LANES)
        span_rows = pl.ds(first, past - first)
        sums.append(
            [
                pltpu.make_async_remote_copy(
                    src_ref=lo_out.at[lax.rem(lo + d, N_LO), :, span_rows], dst_ref=lo_in.at[sender, :, span_rows],
                    send_sem=lo_s.at[p, d], recv_sem=lo_r.at[p, sender], device_id=cells_peer(d), device_id_type=MESH,
                )
                for d in range(N_LO)
            ]
        )
        kept = pltpu.make_async_copy(lo_out.at[lo, :, span_rows], lo_in.at[sender, :, span_rows], lo_r.at[p, sender])
        pl.when(away)(sums[p][0].start)
        pl.when(jnp.logical_not(away))(kept.start)
        for copy in sums[p][1:]:
            copy.start()
    for copy in spreads[0] + spreads[1]:
        copy.wait_send()
    for p, (first, past, _) in enumerate(pieces):
        pl.when(away)(sums[p][0].wait_send)
        for copy in sums[p][1:]:
            copy.wait_send()
        for k in range(N_LO):
            pltpu.make_async_remote_copy(
                src_ref=lo_out.at[k, :, pl.ds(first, past - first)], dst_ref=lo_in.at[k, :, pl.ds(first, past - first)],
                send_sem=lo_s.at[p, k], recv_sem=lo_r.at[p, k], device_id=cells_peer(1), device_id_type=MESH,
            ).wait_recv()
    total = lo_in[0].astype(F32)
    for k in range(1, N_LO):
        total = total + lo_in[k].astype(F32)
    last[...] = (total * (-1.0 / math.sqrt(group * N_LO * N_Y))).reshape(each * SLOT, LANES)
    for c in range(tiles):
        out_ref[:, c * LANES : (c + 1) * LANES] = last[pl.ds(row_of(c), each, stride=SLOT), :]


def body(orbitals, targets, points, fit):
    occupied, shard = orbitals.shape
    targets_n, group = targets.shape[0], points.shape[0]
    each = targets_n // (N_LO * N_Y)
    left, lines, square = tables()
    near, far = N_X * N_CORE - 1, N_HI - 1
    peers = N_GRID - 1
    dma = pltpu.SemaphoreType.DMA
    vmem = pltpu.VMEM
    return pl.pallas_call(
        functools.partial(kernel, occupied, targets_n, group, shard),
        out_shape=jax.ShapeDtypeStruct((each, shard), F32),
        in_specs=[pl.BlockSpec(memory_space=pl.ANY)] * 7,
        out_specs=pl.BlockSpec(memory_space=pltpu.VMEM),
        scratch_shapes=[
            vmem(orbitals.shape, BF16),
            vmem((1, targets_n), jnp.int32),
            vmem((1, group), jnp.int32),
            vmem(fit.shape, F32),
            vmem(left.shape, BF16),
            vmem(lines.shape, BF16),
            vmem(square.shape, F32),
            vmem((group, occupied), BF16),
            vmem((near, group, occupied), BF16),
            vmem((group, occupied), BF16),
            vmem((far, group, occupied), BF16),
            vmem((group, occupied), BF16),
            vmem((group, occupied), BF16),
            vmem(fit.shape, F32),
            vmem(orbitals.shape, BF16),
            vmem((group, shard), F32),
            vmem((N_GRID * SLOT, LANES), F32),
            vmem((N_GRID * shard // 384, 384), BF16),
            vmem((N_GRID * shard // 384, LANES), F32),
            vmem((NG * NG, LANES), F32),
            vmem((NG * NG, LANES), F32),
            vmem((2, 384, 8 * LANES), BF16),
            vmem((N_GRID, SLOT, LANES), BF16),
            vmem((N_GRID, SLOT, LANES), BF16),
            vmem((N_GRID, SLOT, LANES), BF16),
            vmem((N_GRID, SLOT, LANES), BF16),
            vmem((N_Y, targets_n // N_Y, shard), BF16),
            vmem((N_Y - 1, targets_n // N_Y, shard), BF16),
            vmem((N_LO * each * SLOT, LANES), F32),
            vmem((N_LO, each, SLOT, LANES), BF16),
            vmem((N_LO, each, SLOT, LANES), BF16),
            vmem((each * SLOT, LANES), F32),
            dma((near,)), dma((near,)), dma((far,)), dma((far,)),
            dma, dma, dma((N_Y - 1,)), dma((N_Y - 1,)), dma((far,)), dma, dma((far,)), dma,
            dma((peers,)), dma((peers,)), dma((2, peers)), dma((2, peers)),
            dma((2, N_Y - 1)), dma((2, N_Y - 1)), dma((2, N_LO)), dma((2, N_LO)), dma, dma((7,)),
        ],
        compiler_params=pltpu.CompilerParams(collective_id=0, has_side_effects=True, vmem_limit_bytes=60 * 1024 * 1024),
        name="exchange_operator",
    )(
        orbitals, targets.reshape(1, -1), points.reshape(1, -1), fit,
        jnp.asarray(left), jnp.asarray(lines), jnp.asarray(square),
    )


def solution(mesh):
    in_specs = (P(None, "grid"), P(), P("slab"), P("slab", None))
    out_specs = P("slab", "grid")
    return jax.shard_map(body, mesh=mesh, in_specs=in_specs, out_specs=out_specs, check_vma=False)
```

```python
import functools
import math

import jax
import jax.numpy as jnp
import numpy as np
from jax import lax
from jax.experimental import pallas as pl
from jax.experimental.pallas import tpu as pltpu
from jax.sharding import PartitionSpec as P

NG = 48
SCREENING = 4.0
MESH = pl.DeviceIdType.MESH
N_X, N_HI, N_CORE = 4, 4, 2
N_LO, N_Y = 8, 4
N_GRID = N_X * N_HI * N_CORE
LANES = 128
SLOT = 32
PIECE = 16
F32, BF16 = jnp.float32, jnp.bfloat16


def real_basis():
    rows, freq = [], []
    place = np.arange(NG)
    for m in range(NG // 2 + 1):
        scale = math.sqrt((1.0 if m in (0, NG // 2) else 2.0) / NG)
        rows.append(scale * np.cos(2.0 * math.pi * m * place / NG))
        freq.append(m)
    for m in range(1, NG // 2):
        rows.append(math.sqrt(2.0 / NG) * np.sin(2.0 * math.pi * m * place / NG))
        freq.append(m)
    return np.array(rows), np.array(freq)


def split_table(table):
    high = table.astype(BF16)
    low = (table - high.astype(np.float64)).astype(BF16)
    return high, low


def tables():
    basis, freq = real_basis()
    left = []
    for matrix in (basis, basis.T):
        high, low = split_table(matrix)
        left.append(np.concatenate([high, high, low], axis=1))
    lines = np.zeros((2 * NG, LANES), BF16)
    high, low = split_table(basis.T)
    lines[:NG, :NG] = high
    lines[NG:, :NG] = low
    square = ((2.0 * math.pi * freq / NG) ** 2).astype(np.float32)
    column = np.broadcast_to(square[:, None], (NG, LANES)).copy()
    row = np.zeros((8, LANES), np.float32)
    row[:, :NG] = square
    return np.stack(left), lines, np.concatenate([column, row])


def stack(values):
    high = values.astype(BF16)
    low = (values - high.astype(F32)).astype(BF16)
    return jnp.concatenate([high, low, high], axis=0)


def dot(a, b):
    return jnp.dot(a, b, preferred_element_type=F32)


def dot_nt(a, b):
    return lax.dot_general(a, b, (((1,), (1,)), ((), ())), preferred_element_type=F32)


def column_of(row, count):
    same = lax.broadcasted_iota(jnp.int32, (count, count), 0) == lax.broadcasted_iota(jnp.int32, (count, count), 1)
    return jnp.sum(jnp.where(same, row, 0), axis=1, keepdims=True)


def row_of(tile):
    return tile + (tile >= PIECE - 1)


def spans(line):
    return range(line * NG // LANES, (line * NG + NG - 1) // LANES + 1)


def kernel(
    occupied, targets_n, group, shard, orb_hbm, targets_hbm, points_hbm, fit_hbm, left_hbm, lines_hbm, square_hbm,
    out_ref, orb_ref, targets_ref, points_ref, fit_ref, left_ref, lines_ref, square_ref, mine, near, part, far, home_at, task_at, task_fit, task_orb, density, flat, packed, cells, cube, weights, zline,
    send_a, recv_a, send_b, recv_b, y_out, y_in, lo_flat, lo_out, lo_in, last,
    near_s, near_r, far_s, far_r, orb_s, orb_r, all_s, all_r, at_s, at_r, fit_s, fit_r, a_s, a_r, b_s, b_r, y_s, y_r, lo_s, lo_r, local, fetched,
):
    grid, slab = lax.axis_index("grid"), lax.axis_index("slab")
    core, hi, x = lax.rem(grid, N_CORE), lax.rem(grid // N_CORE, N_HI), grid // (N_CORE * N_HI)
    lo, y = slab // N_Y, lax.rem(slab, N_Y)
    tiles = shard // LANES
    rows = tiles // 3
    wire = row_of(tiles - 1) + 1
    pieces = [(0, PIECE, range((PIECE - 1) // 3)), (PIECE, wire, range((PIECE - 1) // 3, rows))]
    each = targets_n // (N_LO * N_Y)

    half, place = lo // N_HI, lax.rem(lo, N_HI)
    at_home = place == hi
    quarter = occupied // N_Y

    def grid_peer(dx, dh, dc):
        return (lax.rem(x + dx, N_X) * N_HI + lax.rem(hi + dh, N_HI)) * N_CORE + lax.rem(core + dc, N_CORE)

    def place_slab(where):
        return (half * N_HI + where) * N_Y + y

    def task_peer(dx, dp, dc):
        return {"grid": grid_peer(dx, 0, dc), "slab": place_slab(lax.rem(place + dp, N_HI))}

    def vector_of(dx, dp, dc):
        return (lax.rem(x + dx, N_X) * N_HI + lax.rem(place + dp, N_HI)) * N_CORE + lax.rem(core + dc, N_CORE)

    vector = vector_of(0, 0, 0)

    def block_of(dx, dp, dc):
        return (lax.rem(x + dx, N_X) * N_HI + lax.rem(place + dp + hi, N_HI)) * N_CORE + lax.rem(core + dc, N_CORE)

    block = block_of(0, 0, 0)
    away = place != 0

    def cells_peer(d):
        return {"grid": grid_peer(0, place, 0), "slab": lax.rem(lo + d, N_LO) * N_Y + y}

    def source_peer(dh, da):
        where = lax.rem(half + da, N_LO // N_HI) * N_HI + lax.rem(N_HI + N_HI - dh, N_HI)
        return {"grid": grid_peer(0, dh, 0), "slab": where * N_Y + y}

    def y_peer(d):
        return lo * N_Y + lax.rem(y + d, N_Y)

    def steps(order):
        return [(dx, d, dc) for ds in order for dx in (2, 1, 3, 0) for dc in (1, 0) for d in ds]

    tasks = [step for step in steps(((2,), (1, 3), (0,))) if any(step)]
    sources = [(dh, da) for dh in range(N_HI) for da in range(N_LO // N_HI)]
    fetches = [
        pltpu.make_async_copy(source, target, fetched.at[i])
        for i, (source, target) in enumerate(
            [
                (points_hbm, points_ref), (orb_hbm, orb_ref), (targets_hbm, targets_ref), (lines_hbm, lines_ref),
                (square_hbm, square_ref), (fit_hbm, fit_ref), (left_hbm, left_ref),
            ]
        )
    ]
    barrier = pltpu.get_barrier_semaphore()

    def hello(peer):
        pl.semaphore_signal(barrier, inc=1, device_id=peer, device_id_type=MESH)

    for d in range(1, N_HI):
        hello({"grid": grid_peer(0, d, 0)})
    for step in sources:
        if any(step):
            hello(source_peer(*step))
    pl.when(away)(lambda: hello(source_peer(0, 0)))
    for step in tasks:
        hello(task_peer(*step))
    for d in range(1, N_Y):
        pl.semaphore_signal(barrier, inc=1, device_id={"slab": y_peer(d)}, device_id_type=MESH)
    for fetch in fetches:
        fetch.start()

    def push(src, dst, send, recv, peer):
        copy = pltpu.make_async_remote_copy(
            src_ref=src, dst_ref=dst, send_sem=send, recv_sem=recv, device_id=peer, device_id_type=MESH
        )
        copy.start()
        return copy

    flat[...] = jnp.zeros_like(flat)
    lo_flat[...] = jnp.zeros_like(lo_flat)
    zline[...] = jnp.zeros_like(zline)
    for fetch in fetches:
        fetch.wait()
    offset = column_of(points_ref[...], group) - grid * shard
    for i in range(rows):
        ids = lax.broadcasted_iota(jnp.int32, (group, 384), 1) + i * 384
        term = dot_nt(
            jnp.where(ids == offset, 1.0, 0.0).astype(BF16), orb_ref[:, i * 384 : (i + 1) * 384]
        )
        total = term if i == 0 else total + term
    mine[...] = total.astype(BF16)
    targets = targets_ref[...]
    occ = lax.broadcasted_iota(jnp.int32, (occupied, targets_n), 0)
    choose = jnp.where(occ == targets, 1.0, 0.0).astype(BF16)
    pick = jnp.where(
        lax.broadcasted_iota(jnp.int32, (targets_n, occupied), 1) == column_of(targets, targets_n), 1.0, 0.0
    ).astype(BF16)
    new = lax.broadcasted_iota(jnp.int32, (targets_n, targets_n), 0)
    old = lax.broadcasted_iota(jnp.int32, (targets_n, targets_n), 1)
    from_old = ((new // each) % N_LO) * (N_Y * each) + (new // (each * N_LO)) * each + new % each
    reorder = dot(jnp.where(old == from_old, 1.0, 0.0).astype(BF16), pick).astype(BF16)
    for line in range(8):
        at = slice(line * NG, (line + 1) * NG)
        for k in range(2):
            zline[k, at, line * LANES : (line + 1) * LANES] = lines_ref[k * NG : (k + 1) * NG, :]
    column, row = square_ref[:NG, :], square_ref[NG : NG + 1, :]

    def weigh(m, carry):
        one = square_ref[pl.ds(m, 1), :]
        weights[pl.ds(pl.multiple_of(m * NG, NG), NG), :] = SCREENING / (SCREENING + column + row + one[:, :1])
        return carry

    lax.fori_loop(0, NG, weigh, 0)
    greetings = N_HI - 1 + len(tasks) + N_LO - 1 + N_Y - 1
    pl.semaphore_wait(barrier, greetings + jnp.where(away, 1, 0))

    own_rows = pl.ds(pl.multiple_of(y * quarter, quarter), quarter)
    lane_pieces = [pl.ds(span[0] * 384, len(span) * 384) for _, _, span in pieces]
    fetch_orb = [
        pltpu.make_async_remote_copy(
            src_ref=orb_ref.at[own_rows, lanes], dst_ref=task_orb.at[own_rows, lanes],
            send_sem=orb_s.at[p], recv_sem=orb_r.at[p],
            device_id={"grid": grid_peer(0, N_HI - place, 0)}, device_id_type=MESH,
        )
        for p, lanes in enumerate(lane_pieces)
    ]
    keep_orb = [
        pltpu.make_async_copy(orb_ref.at[own_rows, lanes], task_orb.at[own_rows, lanes], orb_r.at[p])
        for p, lanes in enumerate(lane_pieces)
    ]

    @pl.when(away)
    def _():
        for copy in fetch_orb:
            copy.start()

    @pl.when(jnp.logical_not(away))
    def _():
        for copy in keep_orb:
            copy.start()

    near_steps = [(dx, 0, dc) for dx in range(N_X) for dc in range(N_CORE) if dx or dc]
    copies = [
        push(mine, near.at[i], near_s.at[i], near_r.at[i], {"grid": grid_peer(*step)})
        for i, step in enumerate(near_steps)
    ]
    for copy in copies:
        copy.wait()
    total = mine[...].astype(F32)
    for i in range(len(near_steps)):
        total = total + near[i].astype(F32)
    part[...] = total.astype(BF16)
    copies = [
        push(part, far.at[d - 1], far_s.at[d - 1], far_r.at[d - 1], {"grid": grid_peer(0, d, 0)})
        for d in range(1, N_HI)
    ]
    for copy in copies:
        copy.wait()
    for i in range(N_HI - 1):
        total = total + far[i].astype(F32)
    at_points = total.astype(BF16)
    home_at[...] = at_points

    def hand(source, target, send, recv):
        return [
            pltpu.make_async_remote_copy(
                src_ref=source, dst_ref=target, send_sem=send.at[d - 1], recv_sem=recv,
                device_id=task_peer(0, d, 0), device_id_type=MESH,
            )
            for d in range(1, N_HI)
        ]

    hands = hand(home_at, task_at, at_s, at_r) + hand(fit_ref, task_fit, fit_s, fit_r)

    @pl.when(at_home)
    def _():
        for copy in hands:
            copy.start()
        task_at[...] = home_at[...]
        task_fit[...] = fit_ref[...]

    copies = []
    for p, lanes in enumerate(lane_pieces):
        fetch_orb[p].wait_recv()
        copies += [
            push(
                task_orb.at[own_rows, lanes], task_orb.at[own_rows, lanes],
                all_s.at[p, d - 1], all_r.at[p, d - 1], {"slab": y_peer(d)},
            )
            for d in range(1, N_Y)
        ]

    @pl.when(jnp.logical_not(at_home))
    def _():
        hands[0].wait_recv()
        hands[-1].wait_recv()

    at_task = task_at[...]
    ordered = dot_nt(reorder, at_task).astype(BF16)
    fit = task_fit[...]
    fit_1 = fit.astype(BF16)
    fit_2 = (fit - fit_1.astype(F32)).astype(BF16)
    fit_3 = (fit - fit_1.astype(F32) - fit_2.astype(F32)).astype(BF16)
    fits = jnp.concatenate([fit_1, fit_1, fit_2, fit_1, fit_2, fit_3], axis=1)
    target_points = dot(at_task, choose).astype(BF16)
    for copy in copies:
        copy.wait_send()

    def arrive(p):
        for d in range(1, N_Y):
            their_rows = pl.ds(pl.multiple_of(lax.rem(y + N_Y - d, N_Y) * quarter, quarter), quarter)
            pltpu.make_async_remote_copy(
                src_ref=task_orb.at[their_rows, lane_pieces[p]], dst_ref=task_orb.at[their_rows, lane_pieces[p]],
                send_sem=all_s.at[p, d - 1], recv_sem=all_r.at[p, d - 1], device_id={"slab": y_peer(d)},
                device_id_type=MESH,
            ).wait_recv()

    copies = []
    for p, (first, past, span) in enumerate(pieces):
        arrive(p)
        for i in span:
            at = slice(i * 384, (i + 1) * 384)
            orb = task_orb[:, at]
            dense = dot(at_task, orb) * (1.0 / math.sqrt(occupied))
            density[:, at] = dense
            chosen = dot(pick, orb).astype(BF16)
            pair = dense * (dot(target_points, chosen) * (1.0 / math.sqrt(targets_n)))
            pair_1 = pair.astype(BF16)
            rest = pair - pair_1.astype(F32)
            pair_2 = rest.astype(BF16)
            pair_3 = (rest - pair_2.astype(F32)).astype(BF16)
            fitted = dot(fits, jnp.concatenate([pair_1, pair_2, pair_1, pair_3, pair_2, pair_1], axis=0))
            for t in range(3):
                flat[pl.ds(row_of(3 * i + t) - first, group, stride=PIECE), :] = fitted[:, t * LANES : (t + 1) * LANES]
        send_a[:, first : first + PIECE, :] = flat[: N_GRID * PIECE, :].reshape(N_GRID, PIECE, LANES).astype(BF16)
        copies.append(
            [
                push(
                    send_a.at[vector_of(*step), pl.ds(first, past - first)],
                    recv_a.at[block, pl.ds(first, past - first)],
                    a_s.at[p, i], a_r.at[p, i], task_peer(*step),
                )
                for i, step in enumerate(tasks)
            ]
        )
    own = pltpu.make_async_copy(send_a.at[vector], recv_a.at[block], local)
    own.start()
    own.wait()
    for p, (first, past, span) in enumerate(pieces):
        for copy in copies[p]:
            copy.wait_recv()
        flat[: N_GRID * PIECE, :] = recv_a[:, first : first + PIECE, :].astype(F32).reshape(N_GRID * PIECE, LANES)
        for i in span:
            for t in range(3):
                packed[i * N_GRID : (i + 1) * N_GRID, t * LANES : (t + 1) * LANES] = flat[
                    pl.ds(row_of(3 * i + t) - first, N_GRID, stride=PIECE), :
                ].astype(BF16)
    for copy in copies[0] + copies[1]:
        copy.wait_send()

    @pl.when(away)
    def _():
        for copy in fetch_orb:
            copy.wait_send()

    @pl.when(at_home)
    def _():
        for copy in hands:
            copy.wait_send()

    for line in range(8):
        at = slice(line * LANES, (line + 1) * LANES)
        got = None
        for t in spans(line):
            lanes = slice(t * LANES, (t + 1) * LANES)
            for k in range(2):
                term = dot(packed[:, lanes], zline[k, lanes, at])
                got = term if got is None else got + term
        for i in range(rows):
            cube[pl.ds(8 * i + line, N_GRID, stride=8 * rows), :] = got[i * N_GRID : (i + 1) * N_GRID, :]

    many = 8

    def pairs_of(values):
        return [jnp.concatenate([stack(a), stack(b)], axis=1) for a, b in zip(values[::2], values[1::2])]

    def apart(values):
        return [v[:, k * LANES : (k + 1) * LANES] for v in values for k in range(2)]

    def along_y(which):
        def one(step, carry):
            at = [pl.ds(pl.multiple_of((step * many + u) * NG, NG), NG) for u in range(many)]
            left = left_ref[which]
            got = apart([dot(left, both) for both in pairs_of([cube[a, :] for a in at])])
            for a, value in zip(at, got):
                cube[a, :] = value
            return carry

        lax.fori_loop(0, NG // many, one, 0)

    def along_x(step, carry):
        at = [pl.ds(step * many + u, NG, stride=NG) for u in range(many)]
        scale = [pl.ds(pl.multiple_of((step * many + u) * NG, NG), NG) for u in range(many)]
        left, back = left_ref[0], left_ref[1]
        got = apart([dot(left, both) for both in pairs_of([cube[a, :] for a in at])])
        got = [value * weights[m, :] for value, m in zip(got, scale)]
        got = apart([dot(back, both) for both in pairs_of(got)])
        for a, value in zip(at, got):
            cube[a, :] = value
        return carry

    along_y(0)
    lax.fori_loop(0, NG // many, along_x, 0)
    along_y(1)
    tile = [None, None, None]
    for line in range(8):
        at = slice(line * LANES, (line + 1) * LANES)
        for i in range(rows):
            cells[i * N_GRID : (i + 1) * N_GRID, :] = cube[pl.ds(8 * i + line, N_GRID, stride=8 * rows), :]
        value = cells[...]
        high = value.astype(BF16)
        low = (value - high.astype(F32)).astype(BF16)
        for t in spans(line):
            lanes = slice(t * LANES, (t + 1) * LANES)
            term = dot_nt(high, zline[0, lanes, at]) + dot_nt(low, zline[0, lanes, at])
            term = term + dot_nt(high, zline[1, lanes, at])
            tile[t] = term if tile[t] is None else tile[t] + term
    for i in range(rows):
        for t in range(3):
            flat[pl.ds(row_of(3 * i + t), N_GRID, stride=SLOT), :] = tile[t][i * N_GRID : (i + 1) * N_GRID, :]
    send_b[...] = flat[...].reshape(N_GRID, SLOT, LANES).astype(BF16)

    spreads = [
        [
            push(
                send_b.at[block_of(*step), pl.ds(first, past - first)],
                recv_b.at[vector, pl.ds(first, past - first)], b_s.at[p, i], b_r.at[p, i], task_peer(*step),
            )
            for i, step in enumerate(tasks)
        ]
        for p, (first, past, _) in enumerate(pieces)
    ]
    own = pltpu.make_async_copy(send_b.at[block], recv_b.at[vector], local)
    own.start()
    own.wait()
    sums, over_y = [], []
    sender = hi * (N_LO // N_HI) + half
    for p, (first, past, span) in enumerate(pieces):
        for copy in spreads[p]:
            copy.wait_recv()
        flat[: N_GRID * PIECE, :] = recv_b[:, first : first + PIECE, :].astype(F32).reshape(N_GRID * PIECE, LANES)
        for i in span:
            at = slice(i * 384, (i + 1) * 384)
            got = [flat[pl.ds(row_of(3 * i + t) - first, group, stride=PIECE), :] for t in range(3)]
            weighted = (jnp.concatenate(got, axis=1) * density[:, at]).astype(BF16)
            y_out[:, :, at] = dot(ordered, weighted).astype(BF16).reshape(N_Y, targets_n // N_Y, 384)
        lanes = lane_pieces[p]
        over_y.append(
            [
                push(
                    y_out.at[lax.rem(y + d, N_Y), :, lanes], y_in.at[d - 1, :, lanes],
                    y_s.at[p, d - 1], y_r.at[p, d - 1], {"slab": y_peer(d)},
                )
                for d in range(1, N_Y)
            ]
        )
    for p, (first, past, span) in enumerate(pieces):
        for copy in over_y[p]:
            copy.wait()
        for i in span:
            at = slice(i * 384, (i + 1) * 384)
            total = y_out[y, :, at].astype(F32)
            for d in range(N_Y - 1):
                total = total + y_in[d, :, at].astype(F32)
            for t in range(3):
                lo_flat[pl.ds(row_of(3 * i + t), N_LO * each, stride=SLOT), :] = total[:, t * LANES : (t + 1) * LANES]
        piece = lo_flat[...].reshape(N_LO * each, SLOT, LANES)[:, first : first + PIECE, :].astype(BF16)
        lo_out[:, :, first : first + PIECE, :] = piece.reshape(N_LO, each, PIECE, LANES)
        span_rows = pl.ds(first, past - first)
        sums.append(
            [
                pltpu.make_async_remote_copy(
                    src_ref=lo_out.at[lax.rem(lo + d, N_LO), :, span_rows], dst_ref=lo_in.at[sender, :, span_rows],
                    send_sem=lo_s.at[p, d], recv_sem=lo_r.at[p, sender], device_id=cells_peer(d), device_id_type=MESH,
                )
                for d in range(N_LO)
            ]
        )
        kept = pltpu.make_async_copy(lo_out.at[lo, :, span_rows], lo_in.at[sender, :, span_rows], lo_r.at[p, sender])
        pl.when(away)(sums[p][0].start)
        pl.when(jnp.logical_not(away))(kept.start)
        for copy in sums[p][1:]:
            copy.start()
    for copy in spreads[0] + spreads[1]:
        copy.wait_send()
    for p, (first, past, _) in enumerate(pieces):
        pl.when(away)(sums[p][0].wait_send)
        for copy in sums[p][1:]:
            copy.wait_send()
        for k in range(N_LO):
            pltpu.make_async_remote_copy(
                src_ref=lo_out.at[k, :, pl.ds(first, past - first)], dst_ref=lo_in.at[k, :, pl.ds(first, past - first)],
                send_sem=lo_s.at[p, k], recv_sem=lo_r.at[p, k], device_id=cells_peer(1), device_id_type=MESH,
            ).wait_recv()
    total = lo_in[0].astype(F32)
    for k in range(1, N_LO):
        total = total + lo_in[k].astype(F32)
    last[...] = (total * (-1.0 / math.sqrt(group * N_LO * N_Y))).reshape(each * SLOT, LANES)
    for c in range(tiles):
        out_ref[:, c * LANES : (c + 1) * LANES] = last[pl.ds(row_of(c), each, stride=SLOT), :]


def body(orbitals, targets, points, fit):
    occupied, shard = orbitals.shape
    targets_n, group = targets.shape[0], points.shape[0]
    each = targets_n // (N_LO * N_Y)
    left, lines, square = tables()
    near, far = N_X * N_CORE - 1, N_HI - 1
    peers = N_GRID - 1
    dma = pltpu.SemaphoreType.DMA
    vmem = pltpu.VMEM
    return pl.pallas_call(
        functools.partial(kernel, occupied, targets_n, group, shard),
        out_shape=jax.ShapeDtypeStruct((each, shard), F32),
        in_specs=[pl.BlockSpec(memory_space=pl.ANY)] * 7,
        out_specs=pl.BlockSpec(memory_space=pltpu.VMEM),
        scratch_shapes=[
            vmem(orbitals.shape, BF16),
            vmem((1, targets_n), jnp.int32),
            vmem((1, group), jnp.int32),
            vmem(fit.shape, F32),
            vmem(left.shape, BF16),
            vmem(lines.shape, BF16),
            vmem(square.shape, F32),
            vmem((group, occupied), BF16),
            vmem((near, group, occupied), BF16),
            vmem((group, occupied), BF16),
            vmem((far, group, occupied), BF16),
            vmem((group, occupied), BF16),
            vmem((group, occupied), BF16),
            vmem(fit.shape, F32),
            vmem(orbitals.shape, BF16),
            vmem((group, shard), F32),
            vmem((N_GRID * SLOT, LANES), F32),
            vmem((N_GRID * shard // 384, 384), BF16),
            vmem((N_GRID * shard // 384, LANES), F32),
            vmem((NG * NG, LANES), F32),
            vmem((NG * NG, LANES), F32),
            vmem((2, 384, 8 * LANES), BF16),
            vmem((N_GRID, SLOT, LANES), BF16),
            vmem((N_GRID, SLOT, LANES), BF16),
            vmem((N_GRID, SLOT, LANES), BF16),
            vmem((N_GRID, SLOT, LANES), BF16),
            vmem((N_Y, targets_n // N_Y, shard), BF16),
            vmem((N_Y - 1, targets_n // N_Y, shard), BF16),
            vmem((N_LO * each * SLOT, LANES), F32),
            vmem((N_LO, each, SLOT, LANES), BF16),
            vmem((N_LO, each, SLOT, LANES), BF16),
            vmem((each * SLOT, LANES), F32),
            dma((near,)), dma((near,)), dma((far,)), dma((far,)),
            dma((2,)), dma((2,)), dma((2, N_Y - 1)), dma((2, N_Y - 1)), dma((far,)), dma, dma((far,)), dma,
            dma((2, peers)), dma((2, peers)), dma((2, peers)), dma((2, peers)),
            dma((2, N_Y - 1)), dma((2, N_Y - 1)), dma((2, N_LO)), dma((2, N_LO)), dma, dma((7,)),
        ],
        compiler_params=pltpu.CompilerParams(collective_id=0, has_side_effects=True, vmem_limit_bytes=60 * 1024 * 1024),
        name="exchange_operator",
    )(
        orbitals, targets.reshape(1, -1), points.reshape(1, -1), fit,
        jnp.asarray(left), jnp.asarray(lines), jnp.asarray(square),
    )


def solution(mesh):
    in_specs = (P(None, "grid"), P(), P("slab"), P("slab", None))
    out_specs = P("slab", "grid")
    return jax.shard_map(body, mesh=mesh, in_specs=in_specs, out_specs=out_specs, check_vma=False)
```

```python
import functools
import math

import jax
import jax.numpy as jnp
import numpy as np
from jax import lax
from jax.experimental import pallas as pl
from jax.experimental.pallas import tpu as pltpu
from jax.sharding import PartitionSpec as P

NG = 48
SCREENING = 4.0
MESH = pl.DeviceIdType.MESH
N_X, N_HI, N_CORE = 4, 4, 2
N_LO, N_Y = 8, 4
N_GRID = N_X * N_HI * N_CORE
LANES = 128
SLOT = 32
PIECE = 16
F32, BF16 = jnp.float32, jnp.bfloat16


def real_basis():
    rows, freq = [], []
    place = np.arange(NG)
    for m in range(NG // 2 + 1):
        scale = math.sqrt((1.0 if m in (0, NG // 2) else 2.0) / NG)
        rows.append(scale * np.cos(2.0 * math.pi * m * place / NG))
        freq.append(m)
    for m in range(1, NG // 2):
        rows.append(math.sqrt(2.0 / NG) * np.sin(2.0 * math.pi * m * place / NG))
        freq.append(m)
    return np.array(rows), np.array(freq)


def split_table(table):
    high = table.astype(BF16)
    low = (table - high.astype(np.float64)).astype(BF16)
    return high, low


def tables():
    basis, freq = real_basis()
    left = []
    for matrix in (basis, basis.T):
        high, low = split_table(matrix)
        left.append(np.concatenate([high, high, low], axis=1))
    lines = np.zeros((2 * NG, LANES), BF16)
    high, low = split_table(basis.T)
    lines[:NG, :NG] = high
    lines[NG:, :NG] = low
    square = ((2.0 * math.pi * freq / NG) ** 2).astype(np.float32)
    column = np.broadcast_to(square[:, None], (NG, LANES)).copy()
    row = np.zeros((8, LANES), np.float32)
    row[:, :NG] = square
    return np.stack(left), lines, np.concatenate([column, row])


def stack(values):
    high = values.astype(BF16)
    low = (values - high.astype(F32)).astype(BF16)
    return jnp.concatenate([high, low, high], axis=0)


def dot(a, b):
    return jnp.dot(a, b, preferred_element_type=F32)


def dot_nt(a, b):
    return lax.dot_general(a, b, (((1,), (1,)), ((), ())), preferred_element_type=F32)


def column_of(row, count):
    same = lax.broadcasted_iota(jnp.int32, (count, count), 0) == lax.broadcasted_iota(jnp.int32, (count, count), 1)
    return jnp.sum(jnp.where(same, row, 0), axis=1, keepdims=True)


def row_of(tile):
    return tile + (tile >= PIECE - 1)


def spans(line):
    return range(line * NG // LANES, (line * NG + NG - 1) // LANES + 1)


def kernel(
    occupied, targets_n, group, shard, orb_hbm, targets_hbm, points_hbm, fit_hbm, left_hbm, lines_hbm, square_hbm,
    out_ref, orb_ref, targets_ref, points_ref, fit_ref, left_ref, lines_ref, square_ref, mine, near, part, far, home_at, task_at, task_fit, task_orb, density, flat, packed, cells, cube, weights, zline,
    send_a, recv_a, send_b, recv_b, y_out, y_in, lo_flat, lo_out, lo_in, last,
    near_s, near_r, far_s, far_r, orb_s, orb_r, all_s, all_r, at_s, at_r, fit_s, fit_r, a_s, a_r, b_s, b_r, y_s, y_r, lo_s, lo_r, local, fetched,
):
    grid, slab = lax.axis_index("grid"), lax.axis_index("slab")
    core, hi, x = lax.rem(grid, N_CORE), lax.rem(grid // N_CORE, N_HI), grid // (N_CORE * N_HI)
    lo, y = slab // N_Y, lax.rem(slab, N_Y)
    tiles = shard // LANES
    rows = tiles // 3
    wire = row_of(tiles - 1) + 1
    pieces = [(0, PIECE, range((PIECE - 1) // 3)), (PIECE, wire, range((PIECE - 1) // 3, rows))]
    each = targets_n // (N_LO * N_Y)

    half, place = lo // N_HI, lax.rem(lo, N_HI)
    at_home = place == hi
    quarter = occupied // N_Y

    def grid_peer(dx, dh, dc):
        return (lax.rem(x + dx, N_X) * N_HI + lax.rem(hi + dh, N_HI)) * N_CORE + lax.rem(core + dc, N_CORE)

    def place_slab(where):
        return (half * N_HI + where) * N_Y + y

    def task_peer(dx, dp, dc):
        return {"grid": grid_peer(dx, 0, dc), "slab": place_slab(lax.rem(place + dp, N_HI))}

    def vector_of(dx, dp, dc):
        return (lax.rem(x + dx, N_X) * N_HI + lax.rem(place + dp, N_HI)) * N_CORE + lax.rem(core + dc, N_CORE)

    vector = vector_of(0, 0, 0)

    def block_of(dx, dp, dc):
        return (lax.rem(x + dx, N_X) * N_HI + lax.rem(place + dp + hi, N_HI)) * N_CORE + lax.rem(core + dc, N_CORE)

    block = block_of(0, 0, 0)
    away = place != 0

    def cells_peer(d):
        return {"grid": grid_peer(0, place, 0), "slab": lax.rem(lo + d, N_LO) * N_Y + y}

    def source_peer(dh, da):
        where = lax.rem(half + da, N_LO // N_HI) * N_HI + lax.rem(N_HI + N_HI - dh, N_HI)
        return {"grid": grid_peer(0, dh, 0), "slab": where * N_Y + y}

    def y_peer(d):
        return lo * N_Y + lax.rem(y + d, N_Y)

    def steps(order):
        return [(dx, d, dc) for ds in order for dx in (2, 1, 3, 0) for dc in (1, 0) for d in ds]

    tasks = [step for step in steps(((2,), (1, 3), (0,))) if any(step)]
    sources = [(dh, da) for dh in range(N_HI) for da in range(N_LO // N_HI)]
    fetches = [
        pltpu.make_async_copy(source, target, fetched.at[i])
        for i, (source, target) in enumerate(
            [
                (points_hbm, points_ref), (orb_hbm, orb_ref), (targets_hbm, targets_ref), (lines_hbm, lines_ref),
                (square_hbm, square_ref), (fit_hbm, fit_ref), (left_hbm, left_ref),
            ]
        )
    ]
    barrier = pltpu.get_barrier_semaphore()

    def hello(peer):
        pl.semaphore_signal(barrier, inc=1, device_id=peer, device_id_type=MESH)

    for d in range(1, N_HI):
        hello({"grid": grid_peer(0, d, 0)})
    for step in sources:
        if any(step):
            hello(source_peer(*step))
    pl.when(away)(lambda: hello(source_peer(0, 0)))
    for step in tasks:
        hello(task_peer(*step))
    for d in range(1, N_Y):
        pl.semaphore_signal(barrier, inc=1, device_id={"slab": y_peer(d)}, device_id_type=MESH)
    for fetch in fetches:
        fetch.start()

    def push(src, dst, send, recv, peer):
        copy = pltpu.make_async_remote_copy(
            src_ref=src, dst_ref=dst, send_sem=send, recv_sem=recv, device_id=peer, device_id_type=MESH
        )
        copy.start()
        return copy

    flat[...] = jnp.zeros_like(flat)
    lo_flat[...] = jnp.zeros_like(lo_flat)
    zline[...] = jnp.zeros_like(zline)
    for fetch in fetches:
        fetch.wait()
    offset = column_of(points_ref[...], group) - grid * shard
    for i in range(rows):
        ids = lax.broadcasted_iota(jnp.int32, (group, 384), 1) + i * 384
        term = dot_nt(
            jnp.where(ids == offset, 1.0, 0.0).astype(BF16), orb_ref[:, i * 384 : (i + 1) * 384]
        )
        total = term if i == 0 else total + term
    mine[...] = total.astype(BF16)
    targets = targets_ref[...]
    occ = lax.broadcasted_iota(jnp.int32, (occupied, targets_n), 0)
    choose = jnp.where(occ == targets, 1.0, 0.0).astype(BF16)
    pick = jnp.where(
        lax.broadcasted_iota(jnp.int32, (targets_n, occupied), 1) == column_of(targets, targets_n), 1.0, 0.0
    ).astype(BF16)
    new = lax.broadcasted_iota(jnp.int32, (targets_n, targets_n), 0)
    old = lax.broadcasted_iota(jnp.int32, (targets_n, targets_n), 1)
    from_old = ((new // each) % N_LO) * (N_Y * each) + (new // (each * N_LO)) * each + new % each
    reorder = dot(jnp.where(old == from_old, 1.0, 0.0).astype(BF16), pick).astype(BF16)
    for line in range(8):
        at = slice(line * NG, (line + 1) * NG)
        for k in range(2):
            zline[k, at, line * LANES : (line + 1) * LANES] = lines_ref[k * NG : (k + 1) * NG, :]
    column, row = square_ref[:NG, :], square_ref[NG : NG + 1, :]

    def weigh(m, carry):
        one = square_ref[pl.ds(m, 1), :]
        weights[pl.ds(pl.multiple_of(m * NG, NG), NG), :] = SCREENING / (SCREENING + column + row + one[:, :1])
        return carry

    lax.fori_loop(0, NG, weigh, 0)
    greetings = N_HI - 1 + len(tasks) + N_LO - 1 + N_Y - 1
    pl.semaphore_wait(barrier, greetings + jnp.where(away, 1, 0))

    own_rows = pl.ds(pl.multiple_of(y * quarter, quarter), quarter)
    lane_pieces = [pl.ds(span[0] * 384, len(span) * 384) for _, _, span in pieces]
    fetch_orb = [
        pltpu.make_async_remote_copy(
            src_ref=orb_ref.at[own_rows, lanes], dst_ref=task_orb.at[own_rows, lanes],
            send_sem=orb_s.at[p], recv_sem=orb_r.at[p],
            device_id={"grid": grid_peer(0, N_HI - place, 0)}, device_id_type=MESH,
        )
        for p, lanes in enumerate(lane_pieces)
    ]
    keep_orb = [
        pltpu.make_async_copy(orb_ref.at[own_rows, lanes], task_orb.at[own_rows, lanes], orb_r.at[p])
        for p, lanes in enumerate(lane_pieces)
    ]

    @pl.when(away)
    def _():
        for copy in fetch_orb:
            copy.start()

    @pl.when(jnp.logical_not(away))
    def _():
        for copy in keep_orb:
            copy.start()

    def hand(source, target, send, recv):
        return [
            pltpu.make_async_remote_copy(
                src_ref=source, dst_ref=target, send_sem=send.at[d - 1], recv_sem=recv,
                device_id=task_peer(0, d, 0), device_id_type=MESH,
            )
            for d in range(1, N_HI)
        ]

    fit_hands = hand(fit_ref, task_fit, fit_s, fit_r)

    @pl.when(at_home)
    def _():
        for copy in fit_hands:
            copy.start()
        task_fit[...] = fit_ref[...]

    near_steps = [(dx, 0, dc) for dx in range(N_X) for dc in range(N_CORE) if dx or dc]
    copies = [
        push(mine, near.at[i], near_s.at[i], near_r.at[i], {"grid": grid_peer(*step)})
        for i, step in enumerate(near_steps)
    ]
    for copy in copies:
        copy.wait()
    total = mine[...].astype(F32)
    for i in range(len(near_steps)):
        total = total + near[i].astype(F32)
    part[...] = total.astype(BF16)
    copies = [
        push(part, far.at[d - 1], far_s.at[d - 1], far_r.at[d - 1], {"grid": grid_peer(0, d, 0)})
        for d in range(1, N_HI)
    ]
    for copy in copies:
        copy.wait()
    for i in range(N_HI - 1):
        total = total + far[i].astype(F32)
    at_points = total.astype(BF16)
    home_at[...] = at_points

    hands = hand(home_at, task_at, at_s, at_r) + fit_hands

    @pl.when(at_home)
    def _():
        for copy in hands[: N_HI - 1]:
            copy.start()
        task_at[...] = home_at[...]

    copies = []
    for p, lanes in enumerate(lane_pieces):
        fetch_orb[p].wait_recv()
        copies += [
            push(
                task_orb.at[own_rows, lanes], task_orb.at[own_rows, lanes],
                all_s.at[p, d - 1], all_r.at[p, d - 1], {"slab": y_peer(d)},
            )
            for d in range(1, N_Y)
        ]

    @pl.when(jnp.logical_not(at_home))
    def _():
        hands[0].wait_recv()
        hands[-1].wait_recv()

    at_task = task_at[...]
    ordered = dot_nt(reorder, at_task).astype(BF16)
    fit = task_fit[...]
    fit_1 = fit.astype(BF16)
    fit_2 = (fit - fit_1.astype(F32)).astype(BF16)
    fit_3 = (fit - fit_1.astype(F32) - fit_2.astype(F32)).astype(BF16)
    fits = jnp.concatenate([fit_1, fit_1, fit_2, fit_1, fit_2, fit_3], axis=1)
    target_points = dot(at_task, choose).astype(BF16)
    for copy in copies:
        copy.wait_send()

    def arrive(p):
        for d in range(1, N_Y):
            their_rows = pl.ds(pl.multiple_of(lax.rem(y + N_Y - d, N_Y) * quarter, quarter), quarter)
            pltpu.make_async_remote_copy(
                src_ref=task_orb.at[their_rows, lane_pieces[p]], dst_ref=task_orb.at[their_rows, lane_pieces[p]],
                send_sem=all_s.at[p, d - 1], recv_sem=all_r.at[p, d - 1], device_id={"slab": y_peer(d)},
                device_id_type=MESH,
            ).wait_recv()

    copies = []
    for p, (first, past, span) in enumerate(pieces):
        arrive(p)
        for i in span:
            at = slice(i * 384, (i + 1) * 384)
            orb = task_orb[:, at]
            dense = dot(at_task, orb) * (1.0 / math.sqrt(occupied))
            density[:, at] = dense
            chosen = dot(pick, orb).astype(BF16)
            pair = dense * (dot(target_points, chosen) * (1.0 / math.sqrt(targets_n)))
            pair_1 = pair.astype(BF16)
            rest = pair - pair_1.astype(F32)
            pair_2 = rest.astype(BF16)
            pair_3 = (rest - pair_2.astype(F32)).astype(BF16)
            fitted = dot(fits, jnp.concatenate([pair_1, pair_2, pair_1, pair_3, pair_2, pair_1], axis=0))
            for t in range(3):
                flat[pl.ds(row_of(3 * i + t) - first, group, stride=PIECE), :] = fitted[:, t * LANES : (t + 1) * LANES]
        send_a[:, first : first + PIECE, :] = flat[: N_GRID * PIECE, :].reshape(N_GRID, PIECE, LANES).astype(BF16)
        copies.append(
            [
                push(
                    send_a.at[vector_of(*step), pl.ds(first, past - first)],
                    recv_a.at[block, pl.ds(first, past - first)],
                    a_s.at[p, i], a_r.at[p, i], task_peer(*step),
                )
                for i, step in enumerate(tasks)
            ]
        )
    own = pltpu.make_async_copy(send_a.at[vector], recv_a.at[block], local)
    own.start()
    own.wait()
    for p, (first, past, span) in enumerate(pieces):
        for copy in copies[p]:
            copy.wait_recv()
        flat[: N_GRID * PIECE, :] = recv_a[:, first : first + PIECE, :].astype(F32).reshape(N_GRID * PIECE, LANES)
        for i in span:
            for t in range(3):
                packed[i * N_GRID : (i + 1) * N_GRID, t * LANES : (t + 1) * LANES] = flat[
                    pl.ds(row_of(3 * i + t) - first, N_GRID, stride=PIECE), :
                ].astype(BF16)
    for copy in copies[0] + copies[1]:
        copy.wait_send()

    @pl.when(away)
    def _():
        for copy in fetch_orb:
            copy.wait_send()

    @pl.when(at_home)
    def _():
        for copy in hands:
            copy.wait_send()

    for line in range(8):
        at = slice(line * LANES, (line + 1) * LANES)
        got = None
        for t in spans(line):
            lanes = slice(t * LANES, (t + 1) * LANES)
            for k in range(2):
                term = dot(packed[:, lanes], zline[k, lanes, at])
                got = term if got is None else got + term
        for i in range(rows):
            cube[pl.ds(8 * i + line, N_GRID, stride=8 * rows), :] = got[i * N_GRID : (i + 1) * N_GRID, :]

    many = 8

    def pairs_of(values):
        return [jnp.concatenate([stack(a), stack(b)], axis=1) for a, b in zip(values[::2], values[1::2])]

    def apart(values):
        return [v[:, k * LANES : (k + 1) * LANES] for v in values for k in range(2)]

    def along_y(which):
        def one(step, carry):
            at = [pl.ds(pl.multiple_of((step * many + u) * NG, NG), NG) for u in range(many)]
            left = left_ref[which]
            got = apart([dot(left, both) for both in pairs_of([cube[a, :] for a in at])])
            for a, value in zip(at, got):
                cube[a, :] = value
            return carry

        lax.fori_loop(0, NG // many, one, 0)

    def along_x(step, carry):
        at = [pl.ds(step * many + u, NG, stride=NG) for u in range(many)]
        scale = [pl.ds(pl.multiple_of((step * many + u) * NG, NG), NG) for u in range(many)]
        left, back = left_ref[0], left_ref[1]
        got = apart([dot(left, both) for both in pairs_of([cube[a, :] for a in at])])
        got = [value * weights[m, :] for value, m in zip(got, scale)]
        got = apart([dot(back, both) for both in pairs_of(got)])
        for a, value in zip(at, got):
            cube[a, :] = value
        return carry

    along_y(0)
    lax.fori_loop(0, NG // many, along_x, 0)
    along_y(1)
    tile = [None, None, None]
    for line in range(8):
        at = slice(line * LANES, (line + 1) * LANES)
        for i in range(rows):
            cells[i * N_GRID : (i + 1) * N_GRID, :] = cube[pl.ds(8 * i + line, N_GRID, stride=8 * rows), :]
        value = cells[...]
        high = value.astype(BF16)
        low = (value - high.astype(F32)).astype(BF16)
        for t in spans(line):
            lanes = slice(t * LANES, (t + 1) * LANES)
            term = dot_nt(high, zline[0, lanes, at]) + dot_nt(low, zline[0, lanes, at])
            term = term + dot_nt(high, zline[1, lanes, at])
            tile[t] = term if tile[t] is None else tile[t] + term
    for i in range(rows):
        for t in range(3):
            flat[pl.ds(row_of(3 * i + t), N_GRID, stride=SLOT), :] = tile[t][i * N_GRID : (i + 1) * N_GRID, :]
    send_b[...] = flat[...].reshape(N_GRID, SLOT, LANES).astype(BF16)

    spreads = [
        [
            push(
                send_b.at[block_of(*step), pl.ds(first, past - first)],
                recv_b.at[vector, pl.ds(first, past - first)], b_s.at[p, i], b_r.at[p, i], task_peer(*step),
            )
            for i, step in enumerate(tasks)
        ]
        for p, (first, past, _) in enumerate(pieces)
    ]
    own = pltpu.make_async_copy(send_b.at[block], recv_b.at[vector], local)
    own.start()
    own.wait()
    sums, over_y = [], []
    sender = hi * (N_LO // N_HI) + half
    for p, (first, past, span) in enumerate(pieces):
        for copy in spreads[p]:
            copy.wait_recv()
        flat[: N_GRID * PIECE, :] = recv_b[:, first : first + PIECE, :].astype(F32).reshape(N_GRID * PIECE, LANES)
        for i in span:
            at = slice(i * 384, (i + 1) * 384)
            got = [flat[pl.ds(row_of(3 * i + t) - first, group, stride=PIECE), :] for t in range(3)]
            weighted = (jnp.concatenate(got, axis=1) * density[:, at]).astype(BF16)
            y_out[:, :, at] = dot(ordered, weighted).astype(BF16).reshape(N_Y, targets_n // N_Y, 384)
        lanes = lane_pieces[p]
        over_y.append(
            [
                push(
                    y_out.at[lax.rem(y + d, N_Y), :, lanes], y_in.at[d - 1, :, lanes],
                    y_s.at[p, d - 1], y_r.at[p, d - 1], {"slab": y_peer(d)},
                )
                for d in range(1, N_Y)
            ]
        )
    for p, (first, past, span) in enumerate(pieces):
        for copy in over_y[p]:
            copy.wait()
        for i in span:
            at = slice(i * 384, (i + 1) * 384)
            total = y_out[y, :, at].astype(F32)
            for d in range(N_Y - 1):
                total = total + y_in[d, :, at].astype(F32)
            for t in range(3):
                lo_flat[pl.ds(row_of(3 * i + t), N_LO * each, stride=SLOT), :] = total[:, t * LANES : (t + 1) * LANES]
        piece = lo_flat[...].reshape(N_LO * each, SLOT, LANES)[:, first : first + PIECE, :].astype(BF16)
        lo_out[:, :, first : first + PIECE, :] = piece.reshape(N_LO, each, PIECE, LANES)
        span_rows = pl.ds(first, past - first)
        sums.append(
            [
                pltpu.make_async_remote_copy(
                    src_ref=lo_out.at[lax.rem(lo + d, N_LO), :, span_rows], dst_ref=lo_in.at[sender, :, span_rows],
                    send_sem=lo_s.at[p, d], recv_sem=lo_r.at[p, sender], device_id=cells_peer(d), device_id_type=MESH,
                )
                for d in range(N_LO)
            ]
        )
        kept = pltpu.make_async_copy(lo_out.at[lo, :, span_rows], lo_in.at[sender, :, span_rows], lo_r.at[p, sender])
        pl.when(away)(sums[p][0].start)
        pl.when(jnp.logical_not(away))(kept.start)
        for copy in sums[p][1:]:
            copy.start()
    for copy in spreads[0] + spreads[1]:
        copy.wait_send()
    for p, (first, past, _) in enumerate(pieces):
        pl.when(away)(sums[p][0].wait_send)
        for copy in sums[p][1:]:
            copy.wait_send()
        for k in range(N_LO):
            pltpu.make_async_remote_copy(
                src_ref=lo_out.at[k, :, pl.ds(first, past - first)], dst_ref=lo_in.at[k, :, pl.ds(first, past - first)],
                send_sem=lo_s.at[p, k], recv_sem=lo_r.at[p, k], device_id=cells_peer(1), device_id_type=MESH,
            ).wait_recv()
    total = lo_in[0].astype(F32)
    for k in range(1, N_LO):
        total = total + lo_in[k].astype(F32)
    last[...] = (total * (-1.0 / math.sqrt(group * N_LO * N_Y))).reshape(each * SLOT, LANES)
    for c in range(tiles):
        out_ref[:, c * LANES : (c + 1) * LANES] = last[pl.ds(row_of(c), each, stride=SLOT), :]


def body(orbitals, targets, points, fit):
    occupied, shard = orbitals.shape
    targets_n, group = targets.shape[0], points.shape[0]
    each = targets_n // (N_LO * N_Y)
    left, lines, square = tables()
    near, far = N_X * N_CORE - 1, N_HI - 1
    peers = N_GRID - 1
    dma = pltpu.SemaphoreType.DMA
    vmem = pltpu.VMEM
    return pl.pallas_call(
        functools.partial(kernel, occupied, targets_n, group, shard),
        out_shape=jax.ShapeDtypeStruct((each, shard), F32),
        in_specs=[pl.BlockSpec(memory_space=pl.ANY)] * 7,
        out_specs=pl.BlockSpec(memory_space=pltpu.VMEM),
        scratch_shapes=[
            vmem(orbitals.shape, BF16),
            vmem((1, targets_n), jnp.int32),
            vmem((1, group), jnp.int32),
            vmem(fit.shape, F32),
            vmem(left.shape, BF16),
            vmem(lines.shape, BF16),
            vmem(square.shape, F32),
            vmem((group, occupied), BF16),
            vmem((near, group, occupied), BF16),
            vmem((group, occupied), BF16),
            vmem((far, group, occupied), BF16),
            vmem((group, occupied), BF16),
            vmem((group, occupied), BF16),
            vmem(fit.shape, F32),
            vmem(orbitals.shape, BF16),
            vmem((group, shard), F32),
            vmem((N_GRID * SLOT, LANES), F32),
            vmem((N_GRID * shard // 384, 384), BF16),
            vmem((N_GRID * shard // 384, LANES), F32),
            vmem((NG * NG, LANES), F32),
            vmem((NG * NG, LANES), F32),
            vmem((2, 384, 8 * LANES), BF16),
            vmem((N_GRID, SLOT, LANES), BF16),
            vmem((N_GRID, SLOT, LANES), BF16),
            vmem((N_GRID, SLOT, LANES), BF16),
            vmem((N_GRID, SLOT, LANES), BF16),
            vmem((N_Y, targets_n // N_Y, shard), BF16),
            vmem((N_Y - 1, targets_n // N_Y, shard), BF16),
            vmem((N_LO * each * SLOT, LANES), F32),
            vmem((N_LO, each, SLOT, LANES), BF16),
            vmem((N_LO, each, SLOT, LANES), BF16),
            vmem((each * SLOT, LANES), F32),
            dma((near,)), dma((near,)), dma((far,)), dma((far,)),
            dma((2,)), dma((2,)), dma((2, N_Y - 1)), dma((2, N_Y - 1)), dma((far,)), dma, dma((far,)), dma,
            dma((2, peers)), dma((2, peers)), dma((2, peers)), dma((2, peers)),
            dma((2, N_Y - 1)), dma((2, N_Y - 1)), dma((2, N_LO)), dma((2, N_LO)), dma, dma((7,)),
        ],
        compiler_params=pltpu.CompilerParams(collective_id=0, has_side_effects=True, vmem_limit_bytes=60 * 1024 * 1024),
        name="exchange_operator",
    )(
        orbitals, targets.reshape(1, -1), points.reshape(1, -1), fit,
        jnp.asarray(left), jnp.asarray(lines), jnp.asarray(square),
    )


def solution(mesh):
    in_specs = (P(None, "grid"), P(), P("slab"), P("slab", None))
    out_specs = P("slab", "grid")
    return jax.shard_map(body, mesh=mesh, in_specs=in_specs, out_specs=out_specs, check_vma=False)
```
